512 devices in a mesh: seq: 64 (over z, y), head: 8 (over x, core).
Axes of the slice: x: 4, y: 8, z: 8, core: 2. Of those that a mesh axis runs over, the one named last changes fastest.
Arguments:
- tokens: bfloat16 [32768, 1024], P('seq'), may hold values from -40 to 40
- w_qkv: bfloat16 [1024, 3072], P(None, 'head'), may hold values from -1 to 1
- w_out: bfloat16 [1024, 1024], P('head'), may hold values from -0.1875 to 0.1875
- offsets: int32 [5, 8], replicated, may hold values from 0 to 15, as said below
Outputs:
- mixed: bfloat16 [32768, 1024], P(('seq', 'head'))
The draws below stay inside these ranges and needn't reach their ends.
Inputs may be any that keep to these rules, and one draw needn't show every extreme that they name: offsets[b, h] lies in 0 .. 2^b - 1.
All inputs are finite; a program needn't handle non-finite values.
Results may differ from the reference program's by a relative error of at most 0.019.
Values may be sent and summed in bfloat16 or wider, within the bound.
A program may use at most 128 MiB of HBM per device.

```python
import math
import jax
import jax.numpy as jnp
from jax import lax

D = 1024
H = 8
HD = 128
NB = 5
TOKENS = 32768
SEG = 2048


def draw_tokens(key, part):
    base = jax.random.truncated_normal(key, -6.0, 6.0, (TOKENS, D), jnp.float32)
    return base.astype(jnp.bfloat16)


def draw_w_qkv(key, part):
    base = jax.random.truncated_normal(key, -6.0, 6.0, (D, H, 3, HD), jnp.float32) / math.sqrt(D)
    return base.reshape(D, 3 * D).astype(jnp.bfloat16)


def draw_offsets(key, part):
    limits = 2 ** jnp.arange(NB, dtype=jnp.int32)
    raw = jax.random.randint(key, (NB, H), 0, 2 ** (NB - 1), dtype=jnp.int32)
    chosen = jax.random.randint(jax.random.fold_in(key, 31), (), 0, H, dtype=jnp.int32)
    column = jnp.arange(H, dtype=jnp.int32)[None, :] == chosen
    return jnp.where(column, limits[:, None] - 1, raw % limits[:, None])


def block_scale(key, shape, cuts, least, top_value):
    loudness = 1.0
    for position, shards_of in cuts:
        steps = jax.random.uniform(jax.random.fold_in(jax.random.fold_in(key, 6), position), (shards_of,), jnp.float32, least / len(cuts), top_value / len(cuts))
        loudness = loudness * jnp.repeat(jnp.exp(steps), shape[position] // shards_of).reshape((-1,) + (1,) * (len(shape) - 1 - position))
    return loudness


def normal_values(key, extent, width, limit, shards=(), held_as=jnp.bfloat16):
    values = jax.random.normal(key, extent, jnp.float32) * width
    if len(shards) > 0:
        values = block_scale(key, extent, shards, -0.22, 0.18) * values
    return jnp.clip(values, min=-limit, max=limit).astype(held_as)


def setup_inputs(seed: int = 0) -> dict:
    arg_keys = jax.random.split(jax.random.key(seed), 5)
    tokens = draw_tokens(jax.random.fold_in(arg_keys[4], 71), 0)
    w_qkv = draw_w_qkv(jax.random.fold_in(arg_keys[4], 71), 0)
    w_out = normal_values(arg_keys[2], (D, D), D ** -0.5, 0.1875, ((0, 8),))
    offsets = draw_offsets(jax.random.fold_in(arg_keys[4], 71), 0)
    return {"tokens": tokens, "w_qkv": w_qkv, "w_out": w_out, "offsets": offsets}


def pick_rows(source_block, offset, stride):
    shaped = source_block.reshape(source_block.shape[0] // stride, stride, source_block.shape[1])
    return lax.dynamic_index_in_dim(shaped, offset, 1, keepdims=False)

def restore(values, offset, stride):
    value_rows = values.shape[0]
    expanded = values[:, None]
    onehot = (jnp.arange(stride, dtype=jnp.int32) == offset).reshape((1, stride) + (1,) * (values.ndim - 1))
    filled = jnp.where(onehot, expanded, jnp.zeros_like(expanded))
    return filled.reshape((value_rows * stride,) + values.shape[1:])

def attend(query, key_values, score_scale):
    head_dim = query.shape[1]
    query32 = query.astype(jnp.float32)
    keys32 = key_values[:, :head_dim].astype(jnp.float32)
    scores = jnp.dot(query32, keys32.T, preferred_element_type=jnp.float32) * score_scale
    row_max = lax.optimization_barrier(jnp.max(scores, axis=1))
    expo = jnp.exp(scores - row_max[:, None])
    row_sum = lax.optimization_barrier(jnp.sum(expo, axis=1))
    weighted = jnp.dot(expo.astype(jnp.bfloat16), key_values[:, head_dim:], preferred_element_type=jnp.float32)
    return (row_max, row_sum, weighted)

def merge_branch(running, row_max, row_sum, weighted, offset, stride):
    max_full = restore(row_max, offset, stride)
    sum_full = restore(row_sum, offset, stride)
    weighted_full = restore(weighted, offset, stride)
    if running is None:
        return (max_full, sum_full, weighted_full)
    run_max, run_sum, summed = running
    selected = jnp.arange(run_max.shape[0], dtype=jnp.int32) % stride == offset
    branch_max = jnp.where(selected, max_full, run_max)
    new_max = jnp.maximum(run_max, branch_max)
    decay_old = jnp.exp(run_max - new_max)
    weight_new = jnp.where(selected, jnp.exp(branch_max - new_max), jnp.zeros_like(new_max))
    run_sum = run_sum * decay_old + weight_new * sum_full
    summed = summed * decay_old[:, None] + weight_new[:, None] * weighted_full
    return (new_max, run_sum, summed)

def reference(tokens, w_qkv, w_out, offsets):
    score_scale = 1.0 / math.sqrt(HD)
    outputs = []
    for head_index in range(H):
        base_col = head_index * 3 * HD
        projected = jnp.dot(tokens, w_qkv[:, base_col:base_col + 3 * HD], preferred_element_type=jnp.float32).astype(jnp.bfloat16)
        queries = projected[:, :HD]
        key_values = projected[:, HD:]
        running = None
        for branch in range(NB):
            stride = 2 ** branch
            offset = offsets[branch, head_index]
            chosen_q = pick_rows(queries, offset, stride)
            chosen_kv = pick_rows(key_values, offset, stride)
            groups = chosen_q.shape[0] // SEG

            def per_segment(operand):
                return attend(operand[0], operand[1], score_scale)
            row_max, row_sum, weighted = lax.map(per_segment, (chosen_q.reshape(groups, SEG, HD), chosen_kv.reshape(groups, SEG, 2 * HD)))
            running = merge_branch(running, row_max.reshape(-1), row_sum.reshape(-1), weighted.reshape(-1, HD), offset, stride)
        run_max, run_sum, summed = running
        outputs.append((summed / run_sum[:, None]).astype(jnp.bfloat16))
    attended = jnp.concatenate(outputs, axis=1)
    return jnp.dot(attended, w_out, preferred_element_type=jnp.float32).astype(jnp.bfloat16)
```

```python
import math

import jax
import jax.numpy as jnp
from jax import lax
from jax.experimental import pallas as pl
from jax.experimental.pallas import tpu as pltpu
from jax.sharding import PartitionSpec as P

HD = 128
NB = 5
RING = 8
LINES = 8
HEADS = 8
ROWS = 512
CHUNKS = 4
CH = ROWS // CHUNKS
RES = 16
PICK = [ROWS >> b for b in range(NB)]
Q4, Q3, Q2 = PICK[4], PICK[3], PICK[2]
QTOT = Q4 + Q3 + Q2
COEF = math.log2(math.e) / math.sqrt(HD)
MESH = pl.DeviceIdType.MESH
BF = jnp.bfloat16
F32 = jnp.float32


BASE = {4: 0, 3: Q4, 2: Q4 + Q3, 1: QTOT}


def prefix(j):
    return QTOT if j == 1 else (Q4 + Q3 if j < 4 else Q4)


def xor(a, j):
    out = 0
    for bit in range(3):
        low = lax.rem(lax.div(a, 1 << bit), 2)
        out = out + ((1 - low) if (j >> bit) & 1 else low) * (1 << bit)
    return out


def home(i):
    g, k = i // 32, i % 32
    res = (g % 2) * 8 + (g // 2 % 2) * 4 + (g // 4 % 2) * 2 + g // 8
    return k * RES + res


def mat(a, b):
    return jnp.dot(a, b, preferred_element_type=F32)


def attend(q, k, v):
    s = lax.dot_general(q, k, (((1,), (1,)), ((), ())), preferred_element_type=F32)
    m = jnp.max(s, axis=1, keepdims=True)
    p = jnp.exp2((s - m) * COEF)
    l = jnp.sum(p, axis=1, keepdims=True)
    return m, l, mat(p.astype(BF), v)


def join(parts):
    top = parts[0][0]
    for m, _, _ in parts[1:]:
        top = jnp.maximum(top, m)
    den, num = 0.0, 0.0
    for m, l, a in parts:
        w = jnp.exp2((m - top) * COEF)
        den = den + w * l
        num = num + w * a
    return top, den, num


def three(x):
    hi = x.astype(BF).astype(F32)
    mid = (x - hi).astype(BF).astype(F32)
    return hi, mid, x - hi - mid


def pack(m, l):
    lane = lax.broadcasted_iota(jnp.int32, (m.shape[0], HD), 1)
    out = jnp.zeros((m.shape[0], HD), F32)
    for i, part in enumerate(three(m) + three(l)):
        out = jnp.where(lane == i, part, out)
    return out.astype(BF)


def unpack(block):
    a = block[:, :HD].astype(F32)
    t = block[:, HD:].astype(F32)
    m = t[:, 0:1] + (t[:, 1:2] + t[:, 2:3])
    l = t[:, 3:4] + (t[:, 4:5] + t[:, 5:6])
    return m, l, a


def kernel(
    off_ref, tok_ref, wqkv_ref, wout_ref, out_ref,
    own, r1, l1, r2, l2, r3, l3, far,
    sel, kb0, kb1, kb2, kb3, kb4, qb, qs, rq, ps, ro, att, ag, wf, acc0, st0,
    ysend, yrecv, qsend, qrecv, psend, precv, wsend, wrecv, asend, arecv,
):
    s_idx = lax.axis_index("seq")
    h = lax.axis_index("head")
    z, y = lax.div(s_idx, RING), lax.rem(s_idx, RING)
    x, core = lax.div(h, 2), lax.rem(h, 2)

    def at_y(d):
        return z * RING + lax.rem(y + RING + d, RING)

    def at_z(j):
        return xor(z, j) * RING + y

    barrier = pltpu.get_barrier_semaphore()
    peers = [(at_y(-1), h), (at_y(1), h)]
    peers += [(at_z(j), h) for j in range(1, LINES)]
    peers += [(s_idx, xor(h, j)) for j in range(1, HEADS)]
    for peer in peers:
        pl.semaphore_signal(barrier, inc=1, device_id=peer, device_id_type=MESH)

    def remote(src, dst, send, recv, peer):
        return pltpu.make_async_remote_copy(
            src_ref=src, dst_ref=dst, send_sem=send, recv_sem=recv,
            device_id=peer, device_id_type=MESH,
        )

    starts = []
    for b in range(1, NB):
        o = off_ref[b, h]
        rev = 0
        for bit in range(b):
            rev = rev * 2 + lax.rem(lax.div(o, 1 << bit), 2)
        starts.append(rev * PICK[b])

    rowi = lax.broadcasted_iota(jnp.int32, (ROWS, ROWS), 0)
    coli = lax.broadcasted_iota(jnp.int32, (ROWS, ROWS), 1)
    perm = jnp.where(home(rowi) == coli, 1.0, 0.0).astype(BF)
    for b in range(NB - 1, 0, -1):
        n = PICK[b]
        hit = rowi[:n] + starts[b - 1] == coli[:n]
        sel[BASE[b] : BASE[b] + n] = jnp.where(hit, 1.0, 0.0).astype(BF)

    kv = mat(tok_ref[...], wqkv_ref[:, HD:]).astype(BF)
    own[...] = mat(perm, kv).astype(BF)
    pl.semaphore_wait(barrier, len(peers))

    flows = [
        ([own, r1, r2, r3], [r1, r2, r3, far], (at_y(-1), h)),
        ([own, l1, l2, l3], [l1, l2, l3, far], (at_y(1), h)),
    ]

    def ring(d, hop, c):
        src, dst, peer = flows[d]
        rows = pl.ds(c * CH, CH)
        return remote(
            src[hop].at[rows], dst[hop].at[rows], ysend.at[d, hop, c], yrecv.at[d, hop, c], peer
        )

    def last(d):
        return range(CHUNKS // 2) if d == 0 else range(CHUNKS // 2, CHUNKS)

    sends = []
    for c in range(CHUNKS):
        for d in range(2):
            copy = ring(d, 0, c)
            copy.start()
            sends.append(copy)

    wcopies = []
    for dx in range(1, 4):
        copy = remote(
            wout_ref, wf.at[h], wsend.at[dx], wrecv.at[dx],
            (s_idx, lax.rem(x + dx, 4) * 2 + core),
        )
        copy.start()
        wcopies.append(copy)
    sibling = (s_idx, x * 2 + 1 - core)
    pair = remote(wout_ref, wf.at[h], wsend.at[0], wrecv.at[0], sibling)
    pair.start()

    q = mat(tok_ref[...], wqkv_ref[:, :HD]).astype(BF)
    qb[...] = mat(perm, q).astype(BF)
    qs[...] = mat(sel[...], qb[...]).astype(BF)
    qcopies = []
    for j in range(1, LINES):
        n = prefix(j)
        copy = remote(
            qs.at[pl.ds(0, n)], rq.at[j, pl.ds(0, n)], qsend.at[j], qrecv.at[j], (at_z(j), h)
        )
        copy.start()
        qcopies.append(copy)
    wf[h] = wout_ref[...]

    def take(ref, slot, place):
        kb0[place] = ref[...]
        taken = mat(sel[...], ref[...]).astype(BF)
        for b, buf in ((1, kb1), (2, kb2), (3, kb3), (4, kb4)):
            n = PICK[b]
            buf[slot * n : (slot + 1) * n] = taken[BASE[b] : BASE[b] + n]

    take(own, 0, y)

    def arrive(hop):
        for c in range(CHUNKS):
            for d in range(2):
                ring(d, hop, c).wait_recv()
                if hop < 2 or c in last(d):
                    copy = ring(d, hop + 1, c)
                    copy.start()
                    sends.append(copy)

    arrive(0)
    take(r1, 1, lax.rem(y + 1, RING))
    take(l1, 2, lax.rem(y + 7, RING))
    arrive(1)
    take(r2, 3, lax.rem(y + 2, RING))
    take(l2, 4, lax.rem(y + 6, RING))

    relays = []
    for dx in range(1, 4):
        wcopies[dx - 1].wait_recv()
        slot = lax.rem(x + 4 - dx, 4) * 2 + core
        copy = remote(wf.at[slot], wf.at[slot], wsend.at[3 + dx], wrecv.at[3 + dx], sibling)
        copy.start()
        relays.append(copy)

    for copy in qcopies:
        copy.wait_recv()
    q1 = qs[QTOT : QTOT + PICK[1]]
    q2 = jnp.concatenate([qs[Q4 + Q3 : QTOT]] + [rq[1, Q4 + Q3 : QTOT]], axis=0)
    q3 = jnp.concatenate([qs[Q4 : Q4 + Q3]] + [rq[j, Q4 : Q4 + Q3] for j in range(1, 4)], axis=0)
    q4 = jnp.concatenate([qs[0:Q4]] + [rq[j, 0:Q4] for j in range(1, LINES)], axis=0)
    small = [(q1, kb1, PICK[1]), (q2, kb2, Q2), (q3, kb3, Q3), (q4, kb4, Q4)]

    arrive(2)
    take(r3, 5, lax.rem(y + 3, RING))
    take(l3, 6, lax.rem(y + 5, RING))
    first = [attend(qq, kb[0 : 7 * n, :HD], kb[0 : 7 * n, HD:]) for qq, kb, n in small]

    for d in range(2):
        for c in last(d):
            ring(d, 3, c).wait_recv()
    take(far, 7, lax.rem(y + 4, RING))
    full = [None] * 4
    for i in (3, 2, 1, 0):
        qq, kb, n = small[i]
        full[i] = join([first[i], attend(qq, kb[7 * n : 8 * n, :HD], kb[7 * n : 8 * n, HD:])])
        if i == 0:
            break
        m, l, a = full[i]
        base = {3: 0, 2: Q4, 1: Q4 + Q3}[i]
        msg = jnp.concatenate([a.astype(BF), pack(m, l)], axis=1)
        for j in range(1, 2 ** i):
            ps[j, base : base + n] = msg[j * n : (j + 1) * n]
        for j in {3: range(4, 8), 2: range(2, 4), 1: range(1, 2)}[i]:
            k = prefix(j)
            copy = remote(
                ps.at[j, pl.ds(0, k)], ro.at[j, pl.ds(0, k)], psend.at[j], precv.at[j], (at_z(j), h)
            )
            copy.start()
            qcopies.append(copy)

    half = lax.div(y, 4) * 4

    def tile(t, carry):
        rows = pl.ds(t * 256, 256)
        keys = kb0[pl.ds(half, 4)].reshape(4 * ROWS, 2 * HD)
        m, l, a = attend(qb[rows, :], keys[:, :HD], keys[:, HD:])
        acc0[rows, :] = a
        st0[0, rows, :] = jnp.broadcast_to(m, (256, HD))
        st0[1, rows, :] = jnp.broadcast_to(l, (256, HD))
        return carry

    lax.fori_loop(0, 2, tile, 0)

    for copy in qcopies[LINES - 1 :]:
        copy.wait_recv()
    own_part = [full[0]]
    for i, base in ((1, Q4 + Q3), (2, Q4), (3, 0)):
        n = PICK[i + 1]
        mine = tuple(v[0:n] for v in full[i])
        own_part.append(join([mine] + [unpack(ro[j, base : base + n]) for j in range(1, 2 ** i)]))

    m0, l0, a0 = st0[0], st0[1], acc0[...]
    rows = lax.broadcasted_iota(jnp.int32, (ROWS, HD), 0)
    spread = []
    top = m0
    for b in range(1, NB):
        m, l, a = own_part[b - 1]
        n = PICK[b]
        chosen = (rows >= starts[b - 1]) & (rows < starts[b - 1] + n)
        m = jnp.broadcast_to(m, (n, HD))
        l = jnp.broadcast_to(l, (n, HD))
        m, l, a = (jnp.concatenate([v] * (2 ** b), axis=0) for v in (m, l, a))
        m = jnp.where(chosen, m, m0)
        top = jnp.maximum(top, m)
        spread.append((chosen, m, l, a))
    w = jnp.exp2((m0 - top) * COEF)
    den, num = w * l0, w * a0
    for chosen, m, l, a in spread:
        w = jnp.where(chosen, jnp.exp2((m - top) * COEF), 0.0)
        den = den + w * l
        num = num + w * a
    attended = (num / den).astype(BF)
    back = jnp.where(home(coli) == rowi, 1.0, 0.0).astype(BF)
    att[...] = mat(back, attended).astype(BF)

    piece = ROWS // HEADS
    acopies = []
    for j in range(1, HEADS):
        to = xor(h, j)
        copy = remote(
            att.at[pl.ds(pl.multiple_of(to * piece, piece), piece)], ag.at[h],
            asend.at[j], arecv.at[j], (s_idx, to),
        )
        copy.start()
        acopies.append(copy)
    ag[h] = att[pl.ds(pl.multiple_of(h * piece, piece), piece), :]
    pair.wait_recv()
    for copy in relays:
        copy.wait_recv()
    for copy in acopies:
        copy.wait_recv()
    lhs = jnp.concatenate([ag[i] for i in range(HEADS)], axis=1)
    out_ref[...] = mat(lhs, wf[...].reshape(HEADS * HD, HEADS * HD)).astype(BF)
    for copy in sends + wcopies + [pair] + relays + qcopies + acopies:
        copy.wait_send()


def on_device(tokens, w_qkv, w_out, offsets):
    vmem = pl.BlockSpec(memory_space=pltpu.VMEM)
    dma = pltpu.SemaphoreType.DMA
    block = pltpu.VMEM((ROWS, 2 * HD), BF)
    return pl.pallas_call(
        kernel,
        out_shape=jax.ShapeDtypeStruct((ROWS // HEADS, HEADS * HD), BF),
        in_specs=[pl.BlockSpec(memory_space=pltpu.SMEM), vmem, vmem, vmem],
        out_specs=vmem,
        scratch_shapes=[block] * 8
        + [pltpu.VMEM((QTOT + PICK[1], ROWS), BF), pltpu.VMEM((RING, ROWS, 2 * HD), BF)]
        + [pltpu.VMEM((RING * PICK[b], 2 * HD), BF) for b in range(1, NB)]
        + [
            pltpu.VMEM((ROWS, HD), BF),
            pltpu.VMEM((QTOT + PICK[1], HD), BF),
            pltpu.VMEM((LINES, QTOT, HD), BF),
            pltpu.VMEM((LINES, QTOT, 2 * HD), BF),
            pltpu.VMEM((LINES, QTOT, 2 * HD), BF),
            pltpu.VMEM((ROWS, HD), BF),
            pltpu.VMEM((HEADS, ROWS // HEADS, HD), BF),
            pltpu.VMEM((HEADS, HD, HEADS * HD), BF),
            pltpu.VMEM((ROWS, HD), F32),
            pltpu.VMEM((2, ROWS, HD), F32),
        ]
        + [dma((2, 4, CHUNKS))] * 2
        + [dma((LINES,))] * 4
        + [dma((7,))] * 2
        + [dma((HEADS,))] * 2,
        compiler_params=pltpu.CompilerParams(
            collective_id=0, has_side_effects=True, vmem_limit_bytes=50 * 1024 * 1024
        ),
    )(offsets, tokens, w_qkv, w_out)


def solution(mesh):
    in_specs = (P("seq", None), P(None, "head"), P("head", None), P())
    out_specs = P(("seq", "head"), None)
    return jax.shard_map(
        on_device, mesh=mesh, in_specs=in_specs, out_specs=out_specs, check_vma=False
    )
```

```python
import math

import jax
import jax.numpy as jnp
from jax import lax
from jax.experimental import pallas as pl
from jax.experimental.pallas import tpu as pltpu
from jax.sharding import PartitionSpec as P

HD = 128
NB = 5
RING = 8
LINES = 8
HEADS = 8
ROWS = 512
RES = 16
BLK = 128
NBLK = ROWS // BLK
HALF = ROWS // 2
CHUNKS = NBLK
CH = HALF // CHUNKS
PICK = [ROWS >> b for b in range(NB)]
PER = [BLK >> b for b in range(NB)]
Q4, Q3, Q2, Q1 = PICK[4], PICK[3], PICK[2], PICK[1]
QTOT = Q4 + Q3 + Q2
BASE = {4: 0, 3: Q4, 2: Q4 + Q3, 1: QTOT}
COEF = math.log2(math.e) / math.sqrt(HD)
MESH = pl.DeviceIdType.MESH
BF = jnp.bfloat16
F32 = jnp.float32
I32 = jnp.int32


def prefix(j):
    return QTOT if j == 1 else (Q4 + Q3 if j < 4 else Q4)


def xor(a, j):
    out = 0
    for bit in range(3):
        low = lax.rem(lax.div(a, 1 << bit), 2)
        out = out + ((1 - low) if (j >> bit) & 1 else low) * (1 << bit)
    return out


def iota(shape, dim):
    return lax.broadcasted_iota(I32, shape, dim)


def home(i):
    g, k = i >> 3, i & 7
    res = ((g & 1) << 3) | ((g & 2) << 1) | ((g & 4) >> 1) | (g >> 3)
    return k * RES + res


def onehot(a, b):
    return jnp.where(a == b, 1.0, 0.0).astype(BF)


def mat(a, b):
    return jnp.dot(a, b, preferred_element_type=F32)


def attend(q, kv):
    s = lax.dot_general(q, kv[:, :HD], (((1,), (1,)), ((), ())), preferred_element_type=F32)
    m = jnp.max(s, axis=1, keepdims=True)
    p = jnp.exp2((s - m) * COEF)
    l = jnp.sum(p, axis=1, keepdims=True)
    return m, l, mat(p.astype(BF), kv[:, HD:])


def join(parts):
    top = parts[0][0]
    for m, _, _ in parts[1:]:
        top = jnp.maximum(top, m)
    den, num = 0.0, 0.0
    for m, l, a in parts:
        w = jnp.exp2((m - top) * COEF)
        den = den + w * l
        num = num + w * a
    return top, den, num


def three(x):
    hi = x.astype(BF).astype(F32)
    mid = (x - hi).astype(BF).astype(F32)
    return hi, mid, x - hi - mid


def pack(m, l):
    lane = iota((m.shape[0], HD), 1)
    out = jnp.zeros((m.shape[0], HD), F32)
    for i, part in enumerate(three(m) + three(l)):
        out = jnp.where(lane == i, part, out)
    return out.astype(BF)


def unpack(block):
    a = block[:, :HD].astype(F32)
    t = block[:, HD:].astype(F32)
    m = t[:, 0:1] + (t[:, 1:2] + t[:, 2:3])
    l = t[:, 3:4] + (t[:, 4:5] + t[:, 5:6])
    return m, l, a


def kernel(
    off_hbm, tok_hbm, wqkv_hbm, wout_hbm, out_ref,
    off, tok, wkv, wq, wout, rings, selq, sela, selb, kb0, kb1, kb2, kb3, kb4, qb, qs, rq, ps, ro,
    att, ag, wf, acc0, st0, res1, res2, res3, res4,
    insem, ysend, yrecv, qsend, qrecv, psend, precv, wsend, wrecv, asend, arecv,
):
    s_idx = lax.axis_index("seq")
    h = lax.axis_index("head")
    z, y = lax.div(s_idx, RING), lax.rem(s_idx, RING)
    x, core = lax.div(h, 2), lax.rem(h, 2)

    loads = [
        (off_hbm, off),
        (wqkv_hbm.at[:, pl.ds(HD, 2 * HD)], wkv),
        *((tok_hbm.at[pl.ds(c * BLK, BLK)], tok.at[pl.ds(c * BLK, BLK)]) for c in range(NBLK)),
        (wqkv_hbm.at[:, pl.ds(0, HD)], wq),
        (wout_hbm, wout),
    ]
    loads = [pltpu.make_async_copy(a, b, insem.at[i]) for i, (a, b) in enumerate(loads)]
    for copy in loads:
        copy.start()

    def at_y(d):
        return z * RING + lax.rem(y + RING + d, RING)

    barrier = pltpu.get_barrier_semaphore()
    peers = [(at_y(-1), h), (at_y(1), h)]
    peers += [(xor(z, j) * RING + y, h) for j in range(1, LINES)]
    peers += [(s_idx, xor(h, j)) for j in range(1, HEADS)]
    for peer in peers:
        pl.semaphore_signal(barrier, inc=1, device_id=peer, device_id_type=MESH)

    def remote(src, dst, send, recv, peer):
        return pltpu.make_async_remote_copy(
            src_ref=src, dst_ref=dst, send_sem=send, recv_sem=recv,
            device_id=peer, device_id_type=MESH,
        )

    loads[0].wait()
    offs = [off[b, h] for b in range(NB)]
    revs = [0]
    for b in range(1, NB):
        rev = 0
        for bit in range(b):
            rev = rev * 2 + lax.rem(lax.div(offs[b], 1 << bit), 2)
        revs.append(rev)
    wanted = []
    for rho in range(RES):
        hit = (offs[4] == rho) | (offs[3] == rho % 8) | (offs[2] == rho % 4)
        wanted.append(jnp.where(hit, 1, 0))
    total = sum(wanted)
    ranks, before = [], 0
    for rho in range(RES):
        ranks.append(before * wanted[rho] + (total + rho - before) * (1 - wanted[rho]))
        before = before + wanted[rho]

    lane = iota((1, BLK), 1)
    rank = jnp.zeros((1, BLK), I32)
    for rho in range(RES):
        rank = jnp.where((lane & 15) == rho, ranks[rho], rank)
    travel = onehot(iota((BLK, 1), 0), rank * 8 + (lane >> 4))
    place = iota((1, ROWS), 1)
    group = ((place >> 3) & 7) + ((place >> 8) << 3)
    label = jnp.zeros((1, ROWS), I32)
    for rho in range(RES):
        label = jnp.where(group == ranks[rho], rho, label)
    label = label * 32 + ((place >> 6) & 3) * 8 + (place & 7)
    for b in range(NB - 1, 0, -1):
        n = PICK[b]
        row = iota((n, 1), 0)
        key = (offs[b] + (row >> 5) * (1 << b)) * 32 + (row & 31)
        if b > 1:
            sela[BASE[b] : BASE[b] + n] = onehot(key, label[:, :HALF])
        else:
            selb[...] = onehot(key, label)
    static = onehot(home(iota((BLK, 1), 0)), iota((1, BLK), 1))
    back = onehot(iota((BLK, 1), 0), home(iota((1, BLK), 1)))

    own, sides, far = 0, [[1, 3, 5], [2, 4, 6]], 7
    flow_peer = [(at_y(-1), h), (at_y(1), h)]

    def ring(ph, d, hop, c):
        slots = [own] + sides[d] + [far]
        rows = pl.ds(c * CH, CH)
        return remote(
            rings.at[ph, slots[hop], rows], rings.at[ph, slots[hop + 1], rows],
            ysend.at[ph, d, hop, c], yrecv.at[ph, d, hop, c], flow_peer[d],
        )

    def last(d):
        return range(CHUNKS // 2) if d == 0 else range(CHUNKS // 2, CHUNKS)

    sends = []

    def send(ph, hop, c):
        for d in range(2):
            if hop < 3 or c in last(d):
                copy = ring(ph, d, hop, c)
                copy.start()
                sends.append(copy)

    def arrive(ph, hop):
        for c in range(CHUNKS):
            for d in range(2):
                if hop < 3 or c in last(d):
                    ring(ph, d, hop, c).wait_recv()
                    if hop < 2 or (hop == 2 and c in last(d)):
                        copy = ring(ph, d, hop + 1, c)
                        copy.start()
                        sends.append(copy)

    loads[1].wait()
    for c in range(NBLK):
        loads[2 + c].wait()
        kv = mat(tok[c * BLK : (c + 1) * BLK], wkv[...]).astype(BF)
        kv = mat(travel, kv).astype(BF)
        rings[0, own, c * CH : (c + 1) * CH] = kv[:CH]
        rings[1, own, c * CH : (c + 1) * CH] = kv[CH:]
        if c == 0:
            pl.semaphore_wait(barrier, len(peers))
        send(0, 0, c)

    loads[6].wait()
    for c in range(NBLK):
        rows = slice(c * BLK, (c + 1) * BLK)
        qb[rows] = mat(static, mat(tok[rows], wq[...]).astype(BF)).astype(BF)
    for b in range(NB - 1, 0, -1):
        n, per = PICK[b], PER[b]
        row = iota((n, 1), 0)
        shift = per.bit_length() - 1
        key = (row >> shift) * BLK + revs[b] * per + (row & (per - 1))
        selq[BASE[b] : BASE[b] + n] = onehot(key, place)
    qs[...] = mat(selq[...], qb[...]).astype(BF)
    qcopies = []
    for j in range(1, LINES):
        n = prefix(j)
        copy = remote(
            qs.at[pl.ds(0, n)], rq.at[j, pl.ds(0, n)], qsend.at[j], qrecv.at[j],
            (xor(z, j) * RING + y, h),
        )
        copy.start()
        qcopies.append(copy)

    loads[7].wait()
    wcopies = []
    for dx in range(1, 4):
        copy = remote(
            wout, wf.at[h], wsend.at[dx], wrecv.at[dx], (s_idx, lax.rem(x + dx, 4) * 2 + core)
        )
        copy.start()
        wcopies.append(copy)
    sibling = (s_idx, x * 2 + 1 - core)
    pair = remote(wout, wf.at[h], wsend.at[0], wrecv.at[0], sibling)
    pair.start()
    wf[h] = wout[...]

    signed = [0, 1, -1, 2, -2, 3, -3, 4]

    def take_a(slot):
        block = rings[0, slot]
        kb0[lax.rem(y + RING + signed[slot], RING), 0:HALF] = block
        taken = mat(sela[...], block).astype(BF)
        for b, buf in ((2, kb2), (3, kb3), (4, kb4)):
            n = PICK[b]
            buf[slot * n : (slot + 1) * n] = taken[BASE[b] : BASE[b] + n]

    def take_b(slot):
        block = rings[1, slot]
        kb0[lax.rem(y + RING + signed[slot], RING), HALF:ROWS] = block
        both = mat(selb[:, :HALF], rings[0, slot]) + mat(selb[:, HALF:], block)
        kb1[slot * Q1 : (slot + 1) * Q1] = both.astype(BF)

    take_a(0)
    arrive(0, 0)
    take_a(1)
    take_a(2)
    arrive(0, 1)
    take_a(3)
    take_a(4)
    arrive(0, 2)
    for c in range(CHUNKS):
        send(1, 0, c)
    take_a(5)
    take_a(6)
    for copy in qcopies:
        copy.wait_recv()
    q1 = qs[QTOT : QTOT + Q1]
    q2 = jnp.concatenate([qs[Q4 + Q3 : QTOT], rq[1, Q4 + Q3 : QTOT]], axis=0)
    q3 = jnp.concatenate([qs[Q4 : Q4 + Q3]] + [rq[j, Q4 : Q4 + Q3] for j in range(1, 4)], axis=0)
    q4 = jnp.concatenate([qs[0:Q4]] + [rq[j, 0:Q4] for j in range(1, LINES)], axis=0)
    arrive(0, 3)
    take_a(far)

    mine = {}
    for b, qq, kb in ((4, q4, kb4), (3, q3, kb3), (2, q2, kb2)):
        m, l, a = attend(qq, kb[...])
        n, base, lines = PICK[b], BASE[b], 1 << (b - 1)
        mine[b] = (m[:n], l[:n], a[:n])
        msg = jnp.concatenate([a.astype(BF), pack(m, l)], axis=1)
        for j in range(1, lines):
            ps[j, base : base + n] = msg[j * n : (j + 1) * n]
        for j in range(lines // 2, lines):
            k = prefix(j)
            copy = remote(
                ps.at[j, pl.ds(0, k)], ro.at[j, pl.ds(0, k)], psend.at[j], precv.at[j],
                (xor(z, j) * RING + y, h),
            )
            copy.start()
            qcopies.append(copy)

    def keep(res, part):
        m, l, a = part
        res[0] = a
        res[1] = jnp.broadcast_to(m, a.shape)
        res[2] = jnp.broadcast_to(l, a.shape)

    take_b(0)
    arrive(1, 0)
    take_b(1)
    take_b(2)
    relays = []
    for dx in range(1, 4):
        wcopies[dx - 1].wait_recv()
        slot = lax.rem(x + 4 - dx, 4) * 2 + core
        copy = remote(wf.at[slot], wf.at[slot], wsend.at[3 + dx], wrecv.at[3 + dx], sibling)
        copy.start()
        relays.append(copy)
    arrive(1, 1)
    take_b(3)
    take_b(4)

    half = lax.div(y, 4) * 4
    upper = lax.div(lax.rem(y, 4), 2)

    def tile(t, carry):
        rows = pl.ds(pl.multiple_of(t * 256, 256), 256)
        keys = kb0[pl.ds(half + upper, 3)].reshape(3 * ROWS, 2 * HD)
        m, l, a = attend(qb[rows, :], keys)
        acc0[rows, :] = a
        st0[0, rows, :] = jnp.broadcast_to(m, (256, HD))
        st0[1, rows, :] = jnp.broadcast_to(l, (256, HD))
        return carry

    def tile2(t, carry):
        rows = pl.ds(pl.multiple_of(t * 256, 256), 256)
        part = attend(qb[rows, :], kb0[half + 3 - 3 * upper])
        m, l, a = join([(st0[0, rows, :], st0[1, rows, :], acc0[rows, :]), part])
        acc0[rows, :] = a
        st0[0, rows, :] = m
        st0[1, rows, :] = l
        return carry

    lax.fori_loop(0, 2, tile, 0)
    first = attend(q1, kb1[0 : 5 * Q1])
    arrive(1, 2)
    take_b(5)
    take_b(6)
    lax.fori_loop(0, 2, tile2, 0)
    second = attend(q1, kb1[5 * Q1 : 7 * Q1])
    for copy in qcopies[LINES - 1 :]:
        copy.wait_recv()
    for b, res in ((2, res2), (3, res3), (4, res4)):
        n, base = PICK[b], BASE[b]
        parts = [unpack(ro[j, base : base + n]) for j in range(1, 1 << (b - 1))]
        keep(res, join([mine[b]] + parts))
    arrive(1, 3)
    take_b(far)
    keep(res1, join([first, second, attend(q1, kb1[7 * Q1 : 8 * Q1])]))

    piece = ROWS // HEADS

    def hand(c, i):
        to = c * 2 + i
        rows = pl.ds(pl.multiple_of(to * piece, piece), piece)
        return remote(att.at[rows], ag.at[h], asend.at[to], arecv.at[h], (s_idx, to))

    def merge(step, carry):
        t = NBLK - 1 - step
        c = lax.rem(x + t + lax.div(t, 2) * (5 - 2 * t), 4)
        rows = pl.ds(pl.multiple_of(c * BLK, BLK), BLK)
        m0, l0, a0 = st0[0, rows, :], st0[1, rows, :], acc0[rows, :]
        place_of = iota((BLK, HD), 0)
        spread = []
        top = m0
        for b, res in ((1, res1), (2, res2), (3, res3), (4, res4)):
            per = PER[b]
            part = pl.ds(pl.multiple_of(c * per, per), per)
            a, m, l = (jnp.concatenate([res[i, part, :]] * (1 << b), axis=0) for i in range(3))
            chosen = (place_of >> (per.bit_length() - 1)) == revs[b]
            m = jnp.where(chosen, m, m0)
            top = jnp.maximum(top, m)
            spread.append((chosen, m, l, a))
        w = jnp.exp2((m0 - top) * COEF)
        den, num = w * l0, w * a0
        for chosen, m, l, a in spread:
            w = jnp.where(chosen, jnp.exp2((m - top) * COEF), 0.0)
            den = den + w * l
            num = num + w * a
        att[rows, :] = mat(back, (num / den).astype(BF)).astype(BF)
        for i in range(2):

            @pl.when(c * 2 + i != h)
            def _():
                hand(c, i).start()

        return carry

    lax.fori_loop(0, NBLK, merge, 0)
    ag[h] = att[pl.ds(pl.multiple_of(h * piece, piece), piece), :]
    pair.wait_recv()
    for copy in relays:
        copy.wait_recv()
    for copy in sends + wcopies + [pair] + relays + qcopies:
        copy.wait_send()
    for j in range(HEADS):

        @pl.when(j != h)
        def _():
            remote(att.at[pl.ds(0, piece)], ag.at[j], asend.at[j], arecv.at[j], (s_idx, j)).wait()

    lhs = jnp.concatenate([ag[i] for i in range(HEADS)], axis=1)
    out_ref[...] = mat(lhs, wf[...].reshape(HEADS * HD, HEADS * HD)).astype(BF)


def on_device(tokens, w_qkv, w_out, offsets):
    hbm = pl.BlockSpec(memory_space=pltpu.HBM)
    dma = pltpu.SemaphoreType.DMA
    vm = pltpu.VMEM
    return pl.pallas_call(
        kernel,
        out_shape=jax.ShapeDtypeStruct((ROWS // HEADS, HEADS * HD), BF),
        in_specs=[hbm] * 4,
        out_specs=pl.BlockSpec(memory_space=pltpu.VMEM),
        scratch_shapes=[
            pltpu.SMEM((NB, HEADS), I32),
            vm((ROWS, HEADS * HD), BF),
            vm((HEADS * HD, 2 * HD), BF),
            vm((HEADS * HD, HD), BF),
            vm((HD, HEADS * HD), BF),
            vm((2, RING, HALF, 2 * HD), BF),
            vm((QTOT + Q1, ROWS), BF),
            vm((QTOT, HALF), BF),
            vm((Q1, ROWS), BF),
            vm((RING, ROWS, 2 * HD), BF),
            *(vm((RING * PICK[b], 2 * HD), BF) for b in range(1, NB)),
            vm((ROWS, HD), BF),
            vm((QTOT + Q1, HD), BF),
            vm((LINES, QTOT, HD), BF),
            vm((LINES, QTOT, 2 * HD), BF),
            vm((LINES, QTOT, 2 * HD), BF),
            vm((ROWS, HD), BF),
            vm((HEADS, ROWS // HEADS, HD), BF),
            vm((HEADS, HD, HEADS * HD), BF),
            vm((ROWS, HD), F32),
            vm((2, ROWS, HD), F32),
            *(vm((3, PICK[b], HD), F32) for b in range(1, NB)),
            dma((8,)),
            dma((2, 2, 4, CHUNKS)),
            dma((2, 2, 4, CHUNKS)),
            *[dma((LINES,))] * 4,
            *[dma((7,))] * 2,
            *[dma((HEADS,))] * 2,
        ],
        compiler_params=pltpu.CompilerParams(
            collective_id=0, has_side_effects=True, vmem_limit_bytes=50 * 1024 * 1024
        ),
    )(offsets, tokens, w_qkv, w_out)


def solution(mesh):
    in_specs = (P("seq", None), P(None, "head"), P("head", None), P())
    out_specs = P(("seq", "head"), None)
    return jax.shard_map(
        on_device, mesh=mesh, in_specs=in_specs, out_specs=out_specs, check_vma=False
    )
```

```python
import math

import jax
import jax.numpy as jnp
from jax import lax
from jax.experimental import pallas as pl
from jax.experimental.pallas import tpu as pltpu
from jax.sharding import PartitionSpec as P

HD = 128
NB = 5
RING = 8
LINES = 8
HEADS = 8
ROWS = 512
RES = 16
BLK = 128
NBLK = ROWS // BLK
HALF = ROWS // 2
CHUNKS = 4
CH = HALF // CHUNKS
PICK = [ROWS >> b for b in range(NB)]
PER = [BLK >> b for b in range(NB)]
Q4, Q3, Q2, Q1 = PICK[4], PICK[3], PICK[2], PICK[1]
QTOT = Q4 + Q3 + Q2
BASE = {4: 0, 3: Q4, 2: Q4 + Q3, 1: QTOT}
COEF = math.log2(math.e) / math.sqrt(HD)
MESH = pl.DeviceIdType.MESH
BF = jnp.bfloat16
F32 = jnp.float32
I32 = jnp.int32


STATS = 16
PBASE = {4: 0, 3: Q4 + STATS, 2: Q4 + Q3 + 2 * STATS}
PTOT = QTOT + 3 * STATS


def prefix(j):
    return QTOT if j == 1 else (Q4 + Q3 if j < 4 else Q4)


def prefix_part(j):
    return PTOT if j == 1 else (PBASE[2] if j < 4 else PBASE[3])


QALL = sum(prefix(j) for j in range(1, LINES))
PALL = sum(prefix_part(j) for j in range(1, LINES))


def xor(a, j):
    out = 0
    for bit in range(3):
        low = lax.rem(lax.div(a, 1 << bit), 2)
        out = out + ((1 - low) if (j >> bit) & 1 else low) * (1 << bit)
    return out


def iota(shape, dim):
    return lax.broadcasted_iota(I32, shape, dim)


def home(i):
    g, k = i >> 3, i & 7
    res = ((g & 1) << 3) | ((g & 2) << 1) | ((g & 4) >> 1) | (g >> 3)
    return k * RES + res


def onehot(a, b):
    return jnp.where(a == b, 1.0, 0.0).astype(BF)


def mat(a, b):
    return jnp.dot(a, b, preferred_element_type=F32)


def attend(q, kv):
    s = lax.dot_general(q, kv[:, :HD], (((1,), (1,)), ((), ())), preferred_element_type=F32)
    m = jnp.max(s, axis=1, keepdims=True)
    p = jnp.exp2((s - m) * COEF)
    l = jnp.sum(p, axis=1, keepdims=True)
    return m, l, mat(p.astype(BF), kv[:, HD:])


def join(parts):
    top = parts[0][0]
    for m, _, _ in parts[1:]:
        top = jnp.maximum(top, m)
    den, num = 0.0, 0.0
    for m, l, a in parts:
        w = jnp.exp2((m - top) * COEF)
        den = den + w * l
        num = num + w * a
    return top, den, num


def three(x):
    hi = x.astype(BF).astype(F32)
    mid = (x - hi).astype(BF).astype(F32)
    return hi, mid, x - hi - mid


def pack(m, l):
    lane = iota((m.shape[0], HD), 1)
    out = jnp.zeros((m.shape[0], HD), F32)
    for i, part in enumerate(three(m) + three(l)):
        out = jnp.where(lane == i, part, out)
    return out.astype(BF)


def turn(a, b):
    return lax.dot_general(a, b, (((1,), (1,)), ((), ())), preferred_element_type=F32)


def unpack(block, n):
    a = block[:n].astype(F32)
    t = turn(onehot(iota((n, 1), 0), iota((1, n), 1)), block[n : n + STATS, :n])
    m = t[:, 0:1] + (t[:, 1:2] + t[:, 2:3])
    l = t[:, 3:4] + (t[:, 4:5] + t[:, 5:6])
    return m, l, a


def kernel(
    off_hbm, tok_hbm, wqkv_hbm, wout_hbm, out_ref,
    off, tok, wkv, wq, wout, rings, selq, sela, selb, kb0, kb1, kb2, kb3, kb4, qb, qs, rq, ps, ro,
    att, ag, wf, spare, acc0, st0, res1, res2, res3, res4,
    insem, ysend, yrecv, zsend, zrecv, wsend, wrecv, asem,
):
    s_idx = lax.axis_index("seq")
    h = lax.axis_index("head")
    z, y = lax.div(s_idx, RING), lax.rem(s_idx, RING)
    x, core = lax.div(h, 2), lax.rem(h, 2)

    loads = [
        (off_hbm, off),
        (wqkv_hbm.at[:, pl.ds(HD, 2 * HD)], wkv),
        *((tok_hbm.at[pl.ds(c * BLK, BLK)], tok.at[pl.ds(c * BLK, BLK)]) for c in range(4)),
        (wqkv_hbm.at[:, pl.ds(0, HD)], wq),
        (wout_hbm, wout),
    ]
    loads = [pltpu.make_async_copy(a, b, insem.at[i]) for i, (a, b) in enumerate(loads)]
    for copy in loads:
        copy.start()

    def at_y(d):
        return z * RING + lax.rem(y + RING + d, RING)

    barrier = pltpu.get_barrier_semaphore()
    peers = [(at_y(-1), h), (at_y(1), h)]
    peers += [(xor(z, j) * RING + y, h) for j in range(1, LINES)]
    peers += [(s_idx, xor(h, j)) for j in range(1, HEADS)]
    for peer in peers:
        pl.semaphore_signal(barrier, inc=1, device_id=peer, device_id_type=MESH)

    def remote(src, dst, send, recv, peer):
        return pltpu.make_async_remote_copy(
            src_ref=src, dst_ref=dst, send_sem=send, recv_sem=recv,
            device_id=peer, device_id_type=MESH,
        )

    loads[0].wait()
    offs = [off[b, h] for b in range(NB)]
    revs = [0]
    for b in range(1, NB):
        rev = 0
        for bit in range(b):
            rev = rev * 2 + lax.rem(lax.div(offs[b], 1 << bit), 2)
        revs.append(rev)
    wanted = []
    for rho in range(RES):
        hit = (offs[4] == rho) | (offs[3] == rho % 8) | (offs[2] == rho % 4)
        wanted.append(jnp.where(hit, 1, 0))
    total = sum(wanted)
    ranks, before = [], 0
    for rho in range(RES):
        ranks.append(before * wanted[rho] + (total + rho - before) * (1 - wanted[rho]))
        before = before + wanted[rho]

    lane = iota((1, BLK), 1)
    rank = jnp.zeros((1, BLK), I32)
    for rho in range(RES):
        rank = jnp.where((lane & 15) == rho, ranks[rho], rank)
    travel = onehot(iota((BLK, 1), 0), rank * 8 + (lane >> 4))

    own, sides, far = 0, [[1, 3, 5], [2, 4, 6]], 7
    flow_peer = [(at_y(-1), h), (at_y(1), h)]

    def ring(ph, d, hop, c):
        slots = [own] + sides[d] + [far]
        rows = pl.ds(c * CH, CH)
        recv = yrecv.at[(ph * 2 + d) * 14 + (hop * CHUNKS + c if hop < 3 else 12 + c % 2)]
        return remote(
            rings.at[ph, slots[hop], rows], rings.at[ph, slots[hop + 1], rows],
            ysend.at[0], recv, flow_peer[d],
        )

    def last(d):
        return range(CHUNKS // 2) if d == 0 else range(CHUNKS // 2, CHUNKS)

    def send(ph, hop, c):
        for d in range(2):
            ring(ph, d, hop, c).start()

    def arrive(ph, hop):
        for c in range(CHUNKS):
            for d in range(2):
                if hop < 3 or c in last(d):
                    ring(ph, d, hop, c).wait_recv()
                    if hop < 2 or (hop == 2 and c in last(d)):
                        ring(ph, d, hop + 1, c).start()

    loads[1].wait()
    for c in range(CHUNKS):
        loads[2 + c].wait()
        kv = mat(tok[c * BLK : (c + 1) * BLK], wkv[...]).astype(BF)
        for i in range(1):
            part = mat(travel, kv[i * BLK : (i + 1) * BLK]).astype(BF)
            at = c * CH + i * (BLK // 2)
            rings[0, own, at : at + BLK // 2] = part[: BLK // 2]
            rings[1, own, at : at + BLK // 2] = part[BLK // 2 :]
        if c == 0:
            pl.semaphore_wait(barrier, len(peers))
        send(0, 0, c)

    place = iota((1, ROWS), 1)
    group = ((place >> 3) & 7) + ((place >> 8) << 3)
    label = jnp.zeros((1, ROWS), I32)
    for rho in range(RES):
        label = jnp.where(group == ranks[rho], rho, label)
    label = label * 32 + ((place >> 6) & 3) * 8 + (place & 7)
    for b in range(NB - 1, 0, -1):
        n = PICK[b]
        row = iota((n, 1), 0)
        key = (offs[b] + (row >> 5) * (1 << b)) * 32 + (row & 31)
        if b > 1:
            sela[BASE[b] : BASE[b] + n] = onehot(key, label[:, :HALF])
        else:
            selb[...] = onehot(key, label)
    static = onehot(home(iota((BLK, 1), 0)), iota((1, BLK), 1))
    back = onehot(iota((BLK, 1), 0), home(iota((1, BLK), 1)))

    loads[6].wait()
    for c in range(NBLK):
        rows = slice(c * BLK, (c + 1) * BLK)
        qb[rows] = mat(static, mat(tok[rows], wq[...]).astype(BF)).astype(BF)
    for b in range(NB - 1, 0, -1):
        n, per = PICK[b], PER[b]
        row = iota((n, 1), 0)
        shift = per.bit_length() - 1
        key = (row >> shift) * BLK + revs[b] * per + (row & (per - 1))
        selq[BASE[b] : BASE[b] + n] = onehot(key, place)
    qs[...] = mat(selq[...], qb[...]).astype(BF)
    for j in range(1, LINES):
        n = prefix(j)
        remote(
            qs.at[pl.ds(0, n)], rq.at[j, pl.ds(0, n)], zsend.at[0], zrecv.at[0],
            (xor(z, j) * RING + y, h),
        ).start()
    qall = remote(spare.at[pl.ds(0, QALL)], spare.at[pl.ds(0, QALL)], zsend.at[0], zrecv.at[0], peers[2])
    pall = remote(spare, spare, zsend.at[1], zrecv.at[1], peers[2])

    loads[7].wait()
    for dx in range(1, 4):
        to = (s_idx, lax.rem(x + dx, 4) * 2 + core)
        remote(wout, wf.at[h], wsend.at[0], wrecv.at[0], to).start()
    sibling = (s_idx, x * 2 + 1 - core)
    remote(wout, wf.at[h], wsend.at[0], wrecv.at[1], sibling).start()
    wf[h] = wout[...]

    def wall(n, sem):
        return remote(wf.at[pl.ds(0, n)], wf.at[pl.ds(0, n)], wsend.at[0], sem, sibling)

    signed = [0, 1, -1, 2, -2, 3, -3, 4]

    def take_a(slot):
        block = rings[0, slot]
        kb0[lax.rem(y + RING + signed[slot], RING), 0:HALF] = block
        taken = mat(sela[...], block).astype(BF)
        for b, buf in ((2, kb2), (3, kb3), (4, kb4)):
            n = PICK[b]
            buf[slot * n : (slot + 1) * n] = taken[BASE[b] : BASE[b] + n]

    def take_b(slot):
        block = rings[1, slot]
        kb0[lax.rem(y + RING + signed[slot], RING), HALF:ROWS] = block
        both = mat(selb[:, :HALF], rings[0, slot]) + mat(selb[:, HALF:], block)
        kb1[slot * Q1 : (slot + 1) * Q1] = both.astype(BF)

    take_a(0)
    arrive(0, 0)
    take_a(1)
    take_a(2)
    arrive(0, 1)
    take_a(3)
    take_a(4)
    arrive(0, 2)
    for c in range(CHUNKS):
        send(1, 0, c)
    take_a(5)
    take_a(6)
    qall.wait_recv()
    q1 = qs[QTOT : QTOT + Q1]
    q2 = jnp.concatenate([qs[Q4 + Q3 : QTOT], rq[1, Q4 + Q3 : QTOT]], axis=0)
    q3 = jnp.concatenate([qs[Q4 : Q4 + Q3]] + [rq[j, Q4 : Q4 + Q3] for j in range(1, 4)], axis=0)
    q4 = jnp.concatenate([qs[0:Q4]] + [rq[j, 0:Q4] for j in range(1, LINES)], axis=0)
    arrive(0, 3)
    take_a(far)

    pick = onehot(iota((STATS, 1), 0), iota((1, HD), 1))
    mine = {}
    for b, qq, kb in ((4, q4, kb4), (3, q3, kb3), (2, q2, kb2)):
        m, l, a = attend(qq, kb[...])
        n, base, lines = PICK[b], PBASE[b], 1 << (b - 1)
        mine[b] = (m[:n], l[:n], a[:n])
        stats = pack(m, l)
        for j in range(1, lines):
            part = slice(j * n, (j + 1) * n)
            ps[j, base : base + n] = a[part].astype(BF)
            ps[j, base + n : base + n + STATS, :n] = turn(pick, stats[part]).astype(BF)
        for j in range(lines // 2, lines):
            k = prefix_part(j)
            remote(
                ps.at[j, pl.ds(0, k)], ro.at[j, pl.ds(0, k)], zsend.at[1], zrecv.at[1],
                (xor(z, j) * RING + y, h),
            ).start()

    def keep(res, part):
        m, l, a = part
        res[0] = a
        res[1] = jnp.broadcast_to(m, a.shape)
        res[2] = jnp.broadcast_to(l, a.shape)

    take_b(0)
    arrive(1, 0)
    take_b(1)
    take_b(2)
    wall(3, wrecv.at[0]).wait_recv()
    for dx in range(1, 4):
        slot = lax.rem(x + 4 - dx, 4) * 2 + core
        remote(wf.at[slot], wf.at[slot], wsend.at[0], wrecv.at[1], sibling).start()
    arrive(1, 1)
    take_b(3)
    take_b(4)

    half = lax.div(y, 4) * 4
    upper = lax.div(lax.rem(y, 4), 2)

    def tile(t, carry):
        rows = pl.ds(pl.multiple_of(t * 256, 256), 256)
        keys = kb0[pl.ds(half + upper, 3)].reshape(3 * ROWS, 2 * HD)
        m, l, a = attend(qb[rows, :], keys)
        acc0[rows, :] = a
        st0[0, rows, :] = jnp.broadcast_to(m, (256, HD))
        st0[1, rows, :] = jnp.broadcast_to(l, (256, HD))
        return carry

    def tile2(t, carry):
        rows = pl.ds(pl.multiple_of(t * 256, 256), 256)
        part = attend(qb[rows, :], kb0[half + 3 - 3 * upper])
        m, l, a = join([(st0[0, rows, :], st0[1, rows, :], acc0[rows, :]), part])
        acc0[rows, :] = a
        st0[0, rows, :] = m
        st0[1, rows, :] = l
        return carry

    lax.fori_loop(0, 2, tile, 0)
    first = attend(q1, kb1[0 : 5 * Q1])
    arrive(1, 2)
    take_b(5)
    take_b(6)
    lax.fori_loop(0, 2, tile2, 0)
    second = attend(q1, kb1[5 * Q1 : 7 * Q1])
    pall.wait_recv()
    for b, res in ((2, res2), (3, res3), (4, res4)):
        n, base = PICK[b], PBASE[b]
        parts = [unpack(ro[j, base : base + n + STATS], n) for j in range(1, 1 << (b - 1))]
        keep(res, join([mine[b]] + parts))
    arrive(1, 3)
    take_b(far)
    keep(res1, join([first, second, attend(q1, kb1[7 * Q1 : 8 * Q1])]))

    piece = ROWS // HEADS

    def hand(c, i):
        to = c * 2 + i
        rows = pl.ds(pl.multiple_of(to * piece, piece), piece)
        return remote(att.at[rows], ag.at[h], asem.at[0], asem.at[1], (s_idx, to))

    def merge(step, carry):
        t = NBLK - 1 - step
        c = lax.rem(x + t + lax.div(t, 2) * (5 - 2 * t), 4)
        rows = pl.ds(pl.multiple_of(c * BLK, BLK), BLK)
        m0, l0, a0 = st0[0, rows, :], st0[1, rows, :], acc0[rows, :]
        place_of = iota((BLK, HD), 0)
        spread = []
        top = m0
        for b, res in ((1, res1), (2, res2), (3, res3), (4, res4)):
            per = PER[b]
            part = pl.ds(pl.multiple_of(c * per, per), per)
            a, m, l = (jnp.concatenate([res[i, part, :]] * (1 << b), axis=0) for i in range(3))
            chosen = (place_of >> (per.bit_length() - 1)) == revs[b]
            m = jnp.where(chosen, m, m0)
            top = jnp.maximum(top, m)
            spread.append((chosen, m, l, a))
        w = jnp.exp2((m0 - top) * COEF)
        den, num = w * l0, w * a0
        for chosen, m, l, a in spread:
            w = jnp.where(chosen, jnp.exp2((m - top) * COEF), 0.0)
            den = den + w * l
            num = num + w * a
        att[rows, :] = mat(back, (num / den).astype(BF)).astype(BF)
        for i in range(2):

            @pl.when(c * 2 + i != h)
            def _():
                hand(c, i).start()

        return carry

    lax.fori_loop(0, NBLK, merge, 0)
    ag[h] = att[pl.ds(pl.multiple_of(h * piece, piece), piece), :]
    wall(4, wrecv.at[1]).wait_recv()
    wall(7, wrecv.at[1]).wait_send()
    qall.wait_send()
    pall.wait_send()
    moved = rings.at[:, pl.ds(0, 7)]
    remote(moved, moved, ysend.at[0], yrecv.at[0], flow_peer[0]).wait_send()
    remote(ag.at[pl.ds(0, 7)], ag.at[pl.ds(0, 7)], asem.at[0], asem.at[1], sibling).wait()

    lhs = jnp.concatenate([ag[i] for i in range(HEADS)], axis=1)
    out_ref[...] = mat(lhs, wf[...].reshape(HEADS * HD, HEADS * HD)).astype(BF)


def on_device(tokens, w_qkv, w_out, offsets):
    hbm = pl.BlockSpec(memory_space=pltpu.HBM)
    dma = pltpu.SemaphoreType.DMA
    vm = pltpu.VMEM
    return pl.pallas_call(
        kernel,
        out_shape=jax.ShapeDtypeStruct((ROWS // HEADS, HEADS * HD), BF),
        in_specs=[hbm] * 4,
        out_specs=pl.BlockSpec(memory_space=pltpu.VMEM),
        scratch_shapes=[
            pltpu.SMEM((NB, HEADS), I32),
            vm((ROWS, HEADS * HD), BF),
            vm((HEADS * HD, 2 * HD), BF),
            vm((HEADS * HD, HD), BF),
            vm((HD, HEADS * HD), BF),
            vm((2, RING, HALF, 2 * HD), BF),
            vm((QTOT + Q1, ROWS), BF),
            vm((QTOT, HALF), BF),
            vm((Q1, ROWS), BF),
            vm((RING, ROWS, 2 * HD), BF),
            *(vm((RING * PICK[b], 2 * HD), BF) for b in range(1, NB)),
            vm((ROWS, HD), BF),
            vm((QTOT + Q1, HD), BF),
            vm((LINES, QTOT, HD), BF),
            vm((LINES, PTOT, HD), BF),
            vm((LINES, PTOT, HD), BF),
            vm((ROWS, HD), BF),
            vm((HEADS, ROWS // HEADS, HD), BF),
            vm((HEADS, HD, HEADS * HD), BF),
            vm((PALL, HD), BF),
            vm((ROWS, HD), F32),
            vm((2, ROWS, HD), F32),
            *(vm((3, PICK[b], HD), F32) for b in range(1, NB)),
            dma((8,)),
            dma((1,)),
            dma((56,)),
            dma((2,)),
            dma((2,)),
            dma((1,)),
            dma((2,)),
            dma((2,)),
        ],
        compiler_params=pltpu.CompilerParams(
            collective_id=0, has_side_effects=True, vmem_limit_bytes=50 * 1024 * 1024
        ),
    )(offsets, tokens, w_qkv, w_out)


def solution(mesh):
    in_specs = (P("seq", None), P(None, "head"), P("head", None), P())
    out_specs = P(("seq", "head"), None)
    return jax.shard_map(
        on_device, mesh=mesh, in_specs=in_specs, out_specs=out_specs, check_vma=False
    )
```

```python
import math

import jax
import jax.numpy as jnp
from jax import lax
from jax.experimental import pallas as pl
from jax.experimental.pallas import tpu as pltpu
from jax.sharding import PartitionSpec as P

HD = 128
NB = 5
RING = 8
LINES = 8
HEADS = 8
ROWS = 512
RES = 16
BLK = 128
NBLK = ROWS // BLK
HALF = ROWS // 2
CHUNKS = 4
CH = HALF // CHUNKS
PICK = [ROWS >> b for b in range(NB)]
PER = [BLK >> b for b in range(NB)]
Q4, Q3, Q2, Q1 = PICK[4], PICK[3], PICK[2], PICK[1]
QTOT = Q4 + Q3 + Q2
BASE = {4: 0, 3: Q4, 2: Q4 + Q3, 1: QTOT}
COEF = math.log2(math.e) / math.sqrt(HD)
MESH = pl.DeviceIdType.MESH
BF = jnp.bfloat16
F32 = jnp.float32
I32 = jnp.int32


STATS = 16
PBASE = {4: 0, 3: Q4 + STATS, 2: Q4 + Q3 + 2 * STATS}
PTOT = QTOT + 3 * STATS


def prefix(j):
    return QTOT if j == 1 else (Q4 + Q3 if j < 4 else Q4)


def prefix_part(j):
    return PTOT if j == 1 else (PBASE[2] if j < 4 else PBASE[3])


QALL = sum(prefix(j) for j in range(1, LINES))
PALL = sum(prefix_part(j) for j in range(1, LINES))


def xor(a, j):
    out = 0
    for bit in range(3):
        low = lax.rem(lax.div(a, 1 << bit), 2)
        out = out + ((1 - low) if (j >> bit) & 1 else low) * (1 << bit)
    return out


def iota(shape, dim):
    return lax.broadcasted_iota(I32, shape, dim)


def home(i):
    g, k = i >> 3, i & 7
    res = ((g & 1) << 3) | ((g & 2) << 1) | ((g & 4) >> 1) | (g >> 3)
    return k * RES + res


def onehot(a, b):
    return jnp.where(a == b, 1.0, 0.0).astype(BF)


def mat(a, b):
    return jnp.dot(a, b, preferred_element_type=F32)


def attend(q, kv):
    s = lax.dot_general(q, kv[:, :HD], (((1,), (1,)), ((), ())), preferred_element_type=F32)
    m = jnp.max(s, axis=1, keepdims=True)
    p = jnp.exp2((s - m) * COEF)
    l = jnp.sum(p, axis=1, keepdims=True)
    return m, l, mat(p.astype(BF), kv[:, HD:])


def join(parts):
    top = parts[0][0]
    for m, _, _ in parts[1:]:
        top = jnp.maximum(top, m)
    den, num = 0.0, 0.0
    for m, l, a in parts:
        w = jnp.exp2((m - top) * COEF)
        den = den + w * l
        num = num + w * a
    return top, den, num


def three(x):
    hi = x.astype(BF).astype(F32)
    mid = (x - hi).astype(BF).astype(F32)
    return hi, mid, x - hi - mid


def pack(m, l):
    lane = iota((m.shape[0], HD), 1)
    out = jnp.zeros((m.shape[0], HD), F32)
    for i, part in enumerate(three(m) + three(l)):
        out = jnp.where(lane == i, part, out)
    return out.astype(BF)


def turn(a, b):
    return lax.dot_general(a, b, (((1,), (1,)), ((), ())), preferred_element_type=F32)


def unpack(block, n):
    a = block[:n].astype(F32)
    t = turn(onehot(iota((n, 1), 0), iota((1, n), 1)), block[n : n + STATS, :n])
    m = t[:, 0:1] + (t[:, 1:2] + t[:, 2:3])
    l = t[:, 3:4] + (t[:, 4:5] + t[:, 5:6])
    return m, l, a


def kernel(
    off_hbm, tok_hbm, wqkv_hbm, wout_hbm, out_ref,
    off, tok, wkv, wq, wout, rings, selq, sela, selb, kb0, kb1, kb2, kb3, kb4, qb, qs, rq, ps, ro,
    att, ag, wf, spare, acc0, st0, res1, res2, res3, res4,
    insem, ysend, yrecv, zsend, zrecv, wsend, wrecv, asem,
):
    s_idx = lax.axis_index("seq")
    h = lax.axis_index("head")
    z, y = lax.div(s_idx, RING), lax.rem(s_idx, RING)
    x, core = lax.div(h, 2), lax.rem(h, 2)

    loads = [
        (off_hbm, off),
        (wqkv_hbm.at[:, pl.ds(HD, 2 * HD)], wkv),
        *((tok_hbm.at[pl.ds(c * BLK, BLK)], tok.at[pl.ds(c * BLK, BLK)]) for c in range(4)),
        (wqkv_hbm.at[:, pl.ds(0, HD)], wq),
        (wout_hbm, wout),
    ]
    loads = [pltpu.make_async_copy(a, b, insem.at[i]) for i, (a, b) in enumerate(loads)]
    for copy in loads:
        copy.start()

    def at_y(d):
        return z * RING + lax.rem(y + RING + d, RING)

    barrier = pltpu.get_barrier_semaphore()
    peers = [(at_y(-1), h), (at_y(1), h)]
    peers += [(xor(z, j) * RING + y, h) for j in range(1, LINES)]
    peers += [(s_idx, xor(h, j)) for j in range(1, HEADS)]
    for peer in peers:
        pl.semaphore_signal(barrier, inc=1, device_id=peer, device_id_type=MESH)

    def remote(src, dst, send, recv, peer):
        return pltpu.make_async_remote_copy(
            src_ref=src, dst_ref=dst, send_sem=send, recv_sem=recv,
            device_id=peer, device_id_type=MESH,
        )

    loads[0].wait()
    offs = [off[b, h] for b in range(NB)]
    revs = [0]
    for b in range(1, NB):
        rev = 0
        for bit in range(b):
            rev = rev * 2 + lax.rem(lax.div(offs[b], 1 << bit), 2)
        revs.append(rev)
    wanted = []
    for rho in range(RES):
        hit = (offs[4] == rho) | (offs[3] == rho % 8) | (offs[2] == rho % 4)
        wanted.append(jnp.where(hit, 1, 0))
    total = sum(wanted)
    ranks, before = [], 0
    for rho in range(RES):
        ranks.append(before * wanted[rho] + (total + rho - before) * (1 - wanted[rho]))
        before = before + wanted[rho]

    lane = iota((1, BLK), 1)
    rank = jnp.zeros((1, BLK), I32)
    for rho in range(RES):
        rank = jnp.where((lane & 15) == rho, ranks[rho], rank)
    travel = onehot(iota((BLK, 1), 0), rank * 8 + (lane >> 4))

    own, sides, far = 0, [[1, 3, 5], [2, 4, 6]], 7
    flow_peer = [(at_y(-1), h), (at_y(1), h)]

    def ring(ph, d, hop, c):
        slots = [own] + sides[d] + [far]
        rows = pl.ds(c * CH, CH)
        recv = yrecv.at[(ph * 2 + d) * 14 + (hop * CHUNKS + c if hop < 3 else 12 + c % 2)]
        return remote(
            rings.at[ph, slots[hop], rows], rings.at[ph, slots[hop + 1], rows],
            ysend.at[0], recv, flow_peer[d],
        )

    def last(d):
        return range(CHUNKS // 2) if d == 0 else range(CHUNKS // 2, CHUNKS)

    def send(ph, hop, c):
        for d in range(2):
            ring(ph, d, hop, c).start()

    def arrive(ph, hop, fill=()):
        for c in range(CHUNKS):
            for d in range(2):
                if hop < 3 or c in last(d):
                    ring(ph, d, hop, c).wait_recv()
                    if hop < 2 or (hop == 2 and c in last(d)):
                        ring(ph, d, hop + 1, c).start()
            if c < len(fill):
                fill[c]()

    loads[1].wait()
    for c in range(CHUNKS):
        loads[2 + c].wait()
        kv = mat(tok[c * BLK : (c + 1) * BLK], wkv[...]).astype(BF)
        for i in range(1):
            part = mat(travel, kv[i * BLK : (i + 1) * BLK]).astype(BF)
            at = c * CH + i * (BLK // 2)
            rings[0, own, at : at + BLK // 2] = part[: BLK // 2]
            rings[1, own, at : at + BLK // 2] = part[BLK // 2 :]
        if c == 0:
            pl.semaphore_wait(barrier, len(peers))
        send(0, 0, c)

    place = iota((1, ROWS), 1)
    group = ((place >> 3) & 7) + ((place >> 8) << 3)
    label = jnp.zeros((1, ROWS), I32)
    for rho in range(RES):
        label = jnp.where(group == ranks[rho], rho, label)
    label = label * 32 + ((place >> 6) & 3) * 8 + (place & 7)
    for b in range(NB - 1, 0, -1):
        n = PICK[b]
        row = iota((n, 1), 0)
        key = (offs[b] + (row >> 5) * (1 << b)) * 32 + (row & 31)
        if b > 1:
            sela[BASE[b] : BASE[b] + n] = onehot(key, label[:, :HALF])
        else:
            selb[...] = onehot(key, label)
    static = onehot(home(iota((BLK, 1), 0)), iota((1, BLK), 1))
    back = onehot(iota((BLK, 1), 0), home(iota((1, BLK), 1)))

    loads[6].wait()
    for c in range(NBLK):
        rows = slice(c * BLK, (c + 1) * BLK)
        qb[rows] = mat(static, mat(tok[rows], wq[...]).astype(BF)).astype(BF)
    for b in range(NB - 1, 0, -1):
        n, per = PICK[b], PER[b]
        row = iota((n, 1), 0)
        shift = per.bit_length() - 1
        key = (row >> shift) * BLK + revs[b] * per + (row & (per - 1))
        selq[BASE[b] : BASE[b] + n] = onehot(key, place)
    qs[...] = mat(selq[...], qb[...]).astype(BF)
    for j in range(1, LINES):
        n = prefix(j)
        remote(
            qs.at[pl.ds(0, n)], rq.at[j, pl.ds(0, n)], zsend.at[0], zrecv.at[0],
            (xor(z, j) * RING + y, h),
        ).start()
    qall = remote(spare.at[pl.ds(0, QALL)], spare.at[pl.ds(0, QALL)], zsend.at[0], zrecv.at[0], peers[2])
    pall = remote(spare, spare, zsend.at[1], zrecv.at[1], peers[2])

    loads[7].wait()
    for dx in range(1, 4):
        to = (s_idx, lax.rem(x + dx, 4) * 2 + core)
        remote(wout, wf.at[h], wsend.at[0], wrecv.at[0], to).start()
    sibling = (s_idx, x * 2 + 1 - core)
    remote(wout, wf.at[h], wsend.at[0], wrecv.at[1], sibling).start()
    wf[h] = wout[...]

    def wall(n, sem):
        return remote(wf.at[pl.ds(0, n)], wf.at[pl.ds(0, n)], wsend.at[0], sem, sibling)

    signed = [0, 1, -1, 2, -2, 3, -3, 4]

    def take_a(slot):
        block = rings[0, slot]
        kb0[lax.rem(y + RING + signed[slot], RING), 0:HALF] = block
        taken = mat(sela[...], block).astype(BF)
        for b, buf in ((2, kb2), (3, kb3), (4, kb4)):
            n = PICK[b]
            buf[slot * n : (slot + 1) * n] = taken[BASE[b] : BASE[b] + n]

    def take_b(slot):
        block = rings[1, slot]
        kb0[lax.rem(y + RING + signed[slot], RING), HALF:ROWS] = block
        both = mat(selb[:, :HALF], rings[0, slot]) + mat(selb[:, HALF:], block)
        kb1[slot * Q1 : (slot + 1) * Q1] = both.astype(BF)

    take_a(0)
    arrive(0, 0)
    take_a(1)
    take_a(2)
    arrive(0, 1)
    take_a(3)
    take_a(4)
    arrive(0, 2)
    for c in range(CHUNKS):
        send(1, 0, c)
    take_a(5)
    take_a(6)
    qall.wait_recv()
    q1 = qs[QTOT : QTOT + Q1]
    q2 = jnp.concatenate([qs[Q4 + Q3 : QTOT], rq[1, Q4 + Q3 : QTOT]], axis=0)
    q3 = jnp.concatenate([qs[Q4 : Q4 + Q3]] + [rq[j, Q4 : Q4 + Q3] for j in range(1, 4)], axis=0)
    q4 = jnp.concatenate([qs[0:Q4]] + [rq[j, 0:Q4] for j in range(1, LINES)], axis=0)
    arrive(0, 3)
    take_a(far)

    pick = onehot(iota((STATS, 1), 0), iota((1, HD), 1))
    mine = {}
    def line(b, qq, kb):
        m, l, a = attend(qq, kb[...])
        n, base, lines = PICK[b], PBASE[b], 1 << (b - 1)
        mine[b] = (m[:n], l[:n], a[:n])
        stats = pack(m, l)
        for j in range(1, lines):
            part = slice(j * n, (j + 1) * n)
            ps[j, base : base + n] = a[part].astype(BF)
            ps[j, base + n : base + n + STATS, :n] = turn(pick, stats[part]).astype(BF)
        for j in range(lines // 2, lines):
            k = prefix_part(j)
            remote(
                ps.at[j, pl.ds(0, k)], ro.at[j, pl.ds(0, k)], zsend.at[1], zrecv.at[1],
                (xor(z, j) * RING + y, h),
            ).start()

    def keep(res, part):
        m, l, a = part
        res[0] = a
        res[1] = jnp.broadcast_to(m, a.shape)
        res[2] = jnp.broadcast_to(l, a.shape)

    lines = [(4, q4, kb4), (3, q3, kb3), (2, q2, kb2)]
    arrive(1, 0, [lambda args=args: line(*args) for args in lines])
    take_b(0)
    take_b(1)
    take_b(2)
    wall(3, wrecv.at[0]).wait_recv()
    for dx in range(1, 4):
        slot = lax.rem(x + 4 - dx, 4) * 2 + core
        remote(wf.at[slot], wf.at[slot], wsend.at[0], wrecv.at[1], sibling).start()
    arrive(1, 1)
    take_b(3)
    take_b(4)

    half = lax.div(y, 4) * 4
    upper = lax.div(lax.rem(y, 4), 2)

    def tile(t, carry):
        rows = pl.ds(pl.multiple_of(t * 256, 256), 256)
        keys = kb0[pl.ds(half + upper, 3)].reshape(3 * ROWS, 2 * HD)
        m, l, a = attend(qb[rows, :], keys)
        acc0[rows, :] = a
        st0[0, rows, :] = jnp.broadcast_to(m, (256, HD))
        st0[1, rows, :] = jnp.broadcast_to(l, (256, HD))
        return carry

    def tile2(t, carry):
        rows = pl.ds(pl.multiple_of(t * 256, 256), 256)
        part = attend(qb[rows, :], kb0[half + 3 - 3 * upper])
        m, l, a = join([(st0[0, rows, :], st0[1, rows, :], acc0[rows, :]), part])
        acc0[rows, :] = a
        st0[0, rows, :] = m
        st0[1, rows, :] = l
        return carry

    first = []
    arrive(
        1, 2,
        [lambda: tile(0, 0), lambda: tile(1, 0), lambda: first.append(attend(q1, kb1[0 : 5 * Q1]))],
    )
    take_b(5)
    take_b(6)
    lax.fori_loop(0, 2, tile2, 0)
    second = attend(q1, kb1[5 * Q1 : 7 * Q1])
    pall.wait_recv()
    for b, res in ((2, res2), (3, res3), (4, res4)):
        n, base = PICK[b], PBASE[b]
        parts = [unpack(ro[j, base : base + n + STATS], n) for j in range(1, 1 << (b - 1))]
        keep(res, join([mine[b]] + parts))
    def blend(rows, c, group):
        m0, l0, a0 = st0[0, rows, :], st0[1, rows, :], acc0[rows, :]
        place_of = iota((BLK, HD), 0)
        spread = []
        top = m0
        for b, res in group:
            per = PER[b]
            part = pl.ds(pl.multiple_of(c * per, per), per)
            a, m, l = (jnp.concatenate([res[i, part, :]] * (1 << b), axis=0) for i in range(3))
            chosen = (place_of >> (per.bit_length() - 1)) == revs[b]
            m = jnp.where(chosen, m, m0)
            top = jnp.maximum(top, m)
            spread.append((chosen, m, l, a))
        w = jnp.exp2((m0 - top) * COEF)
        den, num = w * l0, w * a0
        for chosen, m, l, a in spread:
            w = jnp.where(chosen, jnp.exp2((m - top) * COEF), 0.0)
            den = den + w * l
            num = num + w * a
        return top, den, num

    def premerge(c, carry):
        rows = pl.ds(pl.multiple_of(c * BLK, BLK), BLK)
        top, den, num = blend(rows, c, ((1, res1), (2, res2), (3, res3), (4, res4)))
        st0[0, rows, :] = top
        st0[1, rows, :] = den
        acc0[rows, :] = num
        return carry

    keep(res1, join([first[0], second]))
    lax.fori_loop(0, NBLK, premerge, 0)
    arrive(1, 3)
    take_b(far)
    keep(res1, attend(q1, kb1[7 * Q1 : 8 * Q1]))

    piece = ROWS // HEADS

    def hand(c, i):
        to = c * 2 + i
        rows = pl.ds(pl.multiple_of(to * piece, piece), piece)
        return remote(att.at[rows], ag.at[h], asem.at[0], asem.at[1], (s_idx, to))

    def merge(step, carry):
        t = NBLK - 1 - step
        c = lax.rem(x + t + lax.div(t, 2) * (5 - 2 * t), 4)
        rows = pl.ds(pl.multiple_of(c * BLK, BLK), BLK)
        _, den, num = blend(rows, c, ((1, res1),))
        att[rows, :] = mat(back, (num / den).astype(BF)).astype(BF)
        for i in range(2):

            @pl.when(c * 2 + i != h)
            def _():
                hand(c, i).start()

        return carry

    lax.fori_loop(0, NBLK, merge, 0)
    ag[h] = att[pl.ds(pl.multiple_of(h * piece, piece), piece), :]
    wall(4, wrecv.at[1]).wait_recv()
    wall(7, wrecv.at[1]).wait_send()
    qall.wait_send()
    pall.wait_send()
    moved = rings.at[:, pl.ds(0, 7)]
    remote(moved, moved, ysend.at[0], yrecv.at[0], flow_peer[0]).wait_send()
    remote(ag.at[pl.ds(0, 7)], ag.at[pl.ds(0, 7)], asem.at[0], asem.at[1], sibling).wait()

    lhs = jnp.concatenate([ag[i] for i in range(HEADS)], axis=1)
    out_ref[...] = mat(lhs, wf[...].reshape(HEADS * HD, HEADS * HD)).astype(BF)


def on_device(tokens, w_qkv, w_out, offsets):
    hbm = pl.BlockSpec(memory_space=pltpu.HBM)
    dma = pltpu.SemaphoreType.DMA
    vm = pltpu.VMEM
    return pl.pallas_call(
        kernel,
        out_shape=jax.ShapeDtypeStruct((ROWS // HEADS, HEADS * HD), BF),
        in_specs=[hbm] * 4,
        out_specs=pl.BlockSpec(memory_space=pltpu.VMEM),
        scratch_shapes=[
            pltpu.SMEM((NB, HEADS), I32),
            vm((ROWS, HEADS * HD), BF),
            vm((HEADS * HD, 2 * HD), BF),
            vm((HEADS * HD, HD), BF),
            vm((HD, HEADS * HD), BF),
            vm((2, RING, HALF, 2 * HD), BF),
            vm((QTOT + Q1, ROWS), BF),
            vm((QTOT, HALF), BF),
            vm((Q1, ROWS), BF),
            vm((RING, ROWS, 2 * HD), BF),
            *(vm((RING * PICK[b], 2 * HD), BF) for b in range(1, NB)),
            vm((ROWS, HD), BF),
            vm((QTOT + Q1, HD), BF),
            vm((LINES, QTOT, HD), BF),
            vm((LINES, PTOT, HD), BF),
            vm((LINES, PTOT, HD), BF),
            vm((ROWS, HD), BF),
            vm((HEADS, ROWS // HEADS, HD), BF),
            vm((HEADS, HD, HEADS * HD), BF),
            vm((PALL, HD), BF),
            vm((ROWS, HD), F32),
            vm((2, ROWS, HD), F32),
            *(vm((3, PICK[b], HD), F32) for b in range(1, NB)),
            dma((8,)),
            dma((1,)),
            dma((56,)),
            dma((2,)),
            dma((2,)),
            dma((1,)),
            dma((2,)),
            dma((2,)),
        ],
        compiler_params=pltpu.CompilerParams(
            collective_id=0, has_side_effects=True, vmem_limit_bytes=50 * 1024 * 1024
        ),
    )(*(pltpu.with_memory_space_constraint(v, pltpu.HBM) for v in (offsets, tokens, w_qkv, w_out)))


def solution(mesh):
    in_specs = (P("seq", None), P(None, "head"), P("head", None), P())
    out_specs = P(("seq", "head"), None)
    return jax.shard_map(
        on_device, mesh=mesh, in_specs=in_specs, out_specs=out_specs, check_vma=False
    )
```

```python
import math

import jax
import jax.numpy as jnp
from jax import lax
from jax.experimental import pallas as pl
from jax.experimental.pallas import tpu as pltpu
from jax.sharding import PartitionSpec as P

HD = 128
NB = 5
RING = 8
LINES = 8
HEADS = 8
ROWS = 512
RES = 16
BLK = 128
NBLK = ROWS // BLK
HALF = ROWS // 2
CHUNKS = 4
CH = HALF // CHUNKS
PICK = [ROWS >> b for b in range(NB)]
PER = [BLK >> b for b in range(NB)]
Q4, Q3, Q2, Q1 = PICK[4], PICK[3], PICK[2], PICK[1]
QTOT = Q4 + Q3 + Q2
BASE = {4: 0, 3: Q4, 2: Q4 + Q3, 1: QTOT}
COEF = math.log2(math.e) / math.sqrt(HD)
MESH = pl.DeviceIdType.MESH
BF = jnp.bfloat16
F32 = jnp.float32
I32 = jnp.int32


STATS = 16
PBASE = {4: 0, 3: Q4 + STATS, 2: Q4 + Q3 + 2 * STATS}
PTOT = QTOT + 3 * STATS


def prefix(j):
    return QTOT if j == 1 else (Q4 + Q3 if j < 4 else Q4)


def prefix_part(j):
    return PTOT if j == 1 else (PBASE[2] if j < 4 else PBASE[3])


QALL = sum(prefix(j) for j in range(1, LINES))
PALL = sum(prefix_part(j) for j in range(1, LINES))


def xor(a, j):
    out = 0
    for bit in range(3):
        low = lax.rem(lax.div(a, 1 << bit), 2)
        out = out + ((1 - low) if (j >> bit) & 1 else low) * (1 << bit)
    return out


def iota(shape, dim):
    return lax.broadcasted_iota(I32, shape, dim)


def home(i):
    g, k = i >> 3, i & 7
    res = ((g & 1) << 3) | ((g & 2) << 1) | ((g & 4) >> 1) | (g >> 3)
    return k * RES + res


def onehot(a, b):
    return jnp.where(a == b, 1.0, 0.0).astype(BF)


def mat(a, b):
    return jnp.dot(a, b, preferred_element_type=F32)


def attend(q, kv):
    s = lax.dot_general(q, kv[:, :HD], (((1,), (1,)), ((), ())), preferred_element_type=F32)
    m = jnp.max(s, axis=1, keepdims=True)
    p = jnp.exp2((s - m) * COEF)
    l = jnp.sum(p, axis=1, keepdims=True)
    return m, l, mat(p.astype(BF), kv[:, HD:])


def join(parts):
    top = parts[0][0]
    for m, _, _ in parts[1:]:
        top = jnp.maximum(top, m)
    den, num = 0.0, 0.0
    for m, l, a in parts:
        w = jnp.exp2((m - top) * COEF)
        den = den + w * l
        num = num + w * a
    return top, den, num


def three(x):
    hi = x.astype(BF).astype(F32)
    mid = (x - hi).astype(BF).astype(F32)
    return hi, mid, x - hi - mid


def pack(m, l):
    lane = iota((m.shape[0], HD), 1)
    out = jnp.zeros((m.shape[0], HD), F32)
    for i, part in enumerate(three(m) + three(l)):
        out = jnp.where(lane == i, part, out)
    return out.astype(BF)


def turn(a, b):
    return lax.dot_general(a, b, (((1,), (1,)), ((), ())), preferred_element_type=F32)


def unpack(block, n):
    a = block[:n].astype(F32)
    t = turn(onehot(iota((n, 1), 0), iota((1, n), 1)), block[n : n + STATS, :n])
    m = t[:, 0:1] + (t[:, 1:2] + t[:, 2:3])
    l = t[:, 3:4] + (t[:, 4:5] + t[:, 5:6])
    return m, l, a


def kernel(
    off_hbm, tok_hbm, wqkv_hbm, wout_hbm, out_ref,
    off, tok, wkv, wq, wout, rings, selq, sela, selb, kb0, kb1, kb2, kb3, kb4, qb, qs, rq, ps, ro,
    att, ag, wf, spare, acc0, st0, res1, res2, res3, res4,
    insem, ysend, yrecv, zsend, zrecv, wsend, wrecv, asem,
):
    s_idx = lax.axis_index("seq")
    h = lax.axis_index("head")
    z, y = lax.div(s_idx, RING), lax.rem(s_idx, RING)
    x, core = lax.div(h, 2), lax.rem(h, 2)

    loads = [
        (off_hbm, off),
        (wqkv_hbm.at[:, pl.ds(HD, 2 * HD)], wkv),
        *((tok_hbm.at[pl.ds(c * BLK, BLK)], tok.at[pl.ds(c * BLK, BLK)]) for c in range(4)),
        (wqkv_hbm.at[:, pl.ds(0, HD)], wq),
        (wout_hbm, wout),
    ]
    loads = [pltpu.make_async_copy(a, b, insem.at[i]) for i, (a, b) in enumerate(loads)]
    for copy in loads:
        copy.start()

    def at_y(d):
        return z * RING + lax.rem(y + RING + d, RING)

    barrier = pltpu.get_barrier_semaphore()
    peers = [(at_y(-1), h), (at_y(1), h)]
    peers += [(xor(z, j) * RING + y, h) for j in range(1, LINES)]
    peers += [(s_idx, xor(h, j)) for j in range(1, HEADS)]
    for peer in peers:
        pl.semaphore_signal(barrier, inc=1, device_id=peer, device_id_type=MESH)

    def remote(src, dst, send, recv, peer):
        return pltpu.make_async_remote_copy(
            src_ref=src, dst_ref=dst, send_sem=send, recv_sem=recv,
            device_id=peer, device_id_type=MESH,
        )

    loads[0].wait()
    offs = [off[b, h] for b in range(NB)]
    revs = [0]
    for b in range(1, NB):
        rev = 0
        for bit in range(b):
            rev = rev * 2 + lax.rem(lax.div(offs[b], 1 << bit), 2)
        revs.append(rev)
    wanted = []
    for rho in range(RES):
        hit = (offs[4] == rho) | (offs[3] == rho % 8) | (offs[2] == rho % 4)
        wanted.append(jnp.where(hit, 1, 0))
    total = sum(wanted)
    ranks, before = [], 0
    for rho in range(RES):
        ranks.append(before * wanted[rho] + (total + rho - before) * (1 - wanted[rho]))
        before = before + wanted[rho]

    lane = iota((1, BLK), 1)
    rank = jnp.zeros((1, BLK), I32)
    for rho in range(RES):
        rank = jnp.where((lane & 15) == rho, ranks[rho], rank)
    travel = onehot(iota((BLK, 1), 0), rank * 8 + (lane >> 4))

    own, sides, far = 0, [[1, 3, 5], [2, 4, 6]], 7
    flow_peer = [(at_y(-1), h), (at_y(1), h)]

    def ring(ph, d, hop, c):
        slots = [own] + sides[d] + [far]
        rows = pl.ds(c * CH, CH)
        recv = yrecv.at[(ph * 2 + d) * 14 + (hop * CHUNKS + c if hop < 3 else 12 + c % 2)]
        return remote(
            rings.at[ph, slots[hop], rows], rings.at[ph, slots[hop + 1], rows],
            ysend.at[0], recv, flow_peer[d],
        )

    def last(d):
        return range(CHUNKS // 2) if d == 0 else range(CHUNKS // 2, CHUNKS)

    def send(ph, hop, c):
        for d in range(2):
            ring(ph, d, hop, c).start()

    def arrive(ph, hop, fill=()):
        for c in range(CHUNKS):
            for d in range(2):
                if hop < 3 or c in last(d):
                    ring(ph, d, hop, c).wait_recv()
                    if hop < 2 or (hop == 2 and c in last(d)):
                        ring(ph, d, hop + 1, c).start()
            if c < len(fill):
                fill[c]()

    loads[1].wait()
    for c in range(CHUNKS):
        loads[2 + c].wait()
        kv = mat(tok[c * BLK : (c + 1) * BLK], wkv[...]).astype(BF)
        for i in range(1):
            part = mat(travel, kv[i * BLK : (i + 1) * BLK]).astype(BF)
            at = c * CH + i * (BLK // 2)
            rings[0, own, at : at + BLK // 2] = part[: BLK // 2]
            rings[1, own, at : at + BLK // 2] = part[BLK // 2 :]
        if c == 0:
            pl.semaphore_wait(barrier, len(peers))
        send(0, 0, c)

    place = iota((1, ROWS), 1)
    group = ((place >> 3) & 7) + ((place >> 8) << 3)
    label = jnp.zeros((1, ROWS), I32)
    for rho in range(RES):
        label = jnp.where(group == ranks[rho], rho, label)
    label = label * 32 + ((place >> 6) & 3) * 8 + (place & 7)
    for b in range(NB - 1, 0, -1):
        n = PICK[b]
        row = iota((n, 1), 0)
        key = (offs[b] + (row >> 5) * (1 << b)) * 32 + (row & 31)
        if b > 1:
            sela[BASE[b] : BASE[b] + n] = onehot(key, label[:, :HALF])
        else:
            selb[...] = onehot(key, label)
    static = onehot(home(iota((BLK, 1), 0)), iota((1, BLK), 1))
    back = onehot(iota((BLK, 1), 0), home(iota((1, BLK), 1)))

    loads[6].wait()
    for c in range(NBLK):
        rows = slice(c * BLK, (c + 1) * BLK)
        qb[rows] = mat(static, mat(tok[rows], wq[...]).astype(BF)).astype(BF)
    for b in range(NB - 1, 0, -1):
        n, per = PICK[b], PER[b]
        row = iota((n, 1), 0)
        shift = per.bit_length() - 1
        key = (row >> shift) * BLK + revs[b] * per + (row & (per - 1))
        selq[BASE[b] : BASE[b] + n] = onehot(key, place)
    qs[...] = mat(selq[...], qb[...]).astype(BF)
    for j in range(1, LINES):
        n = prefix(j)
        remote(
            qs.at[pl.ds(0, n)], rq.at[j, pl.ds(0, n)], zsend.at[0], zrecv.at[0],
            (xor(z, j) * RING + y, h),
        ).start()
    qall = remote(spare.at[pl.ds(0, QALL)], spare.at[pl.ds(0, QALL)], zsend.at[0], zrecv.at[0], peers[2])
    pall = remote(spare, spare, zsend.at[1], zrecv.at[1], peers[2])

    signed = [0, 1, -1, 2, -2, 3, -3, 4]

    def take_a(slot):
        block = rings[0, slot]
        if slot != far:
            kb0[lax.rem(y + RING + signed[slot], RING), 0:HALF] = block
        taken = mat(sela[...], block).astype(BF)
        for b, buf in ((2, kb2), (3, kb3), (4, kb4)):
            n = PICK[b]
            buf[slot * n : (slot + 1) * n] = taken[BASE[b] : BASE[b] + n]

    def take_b(slot):
        block = rings[1, slot]
        if slot != far:
            kb0[lax.rem(y + RING + signed[slot], RING), HALF:ROWS] = block
        both = mat(selb[:, :HALF], rings[0, slot]) + mat(selb[:, HALF:], block)
        if slot == far:
            return both.astype(BF)
        kb1[slot * Q1 : (slot + 1) * Q1] = both.astype(BF)

    arrive(0, 0)

    loads[7].wait()
    for dx in range(1, 4):
        to = (s_idx, lax.rem(x + dx, 4) * 2 + core)
        remote(wout, wf.at[h], wsend.at[0], wrecv.at[0], to).start()
    sibling = (s_idx, x * 2 + 1 - core)
    remote(wout, wf.at[h], wsend.at[0], wrecv.at[1], sibling).start()
    wf[h] = wout[...]

    def wall(n, sem):
        return remote(wf.at[pl.ds(0, n)], wf.at[pl.ds(0, n)], wsend.at[0], sem, sibling)

    take_a(0)
    take_a(1)
    take_a(2)
    arrive(0, 1)
    take_a(3)
    take_a(4)
    arrive(0, 2)
    for c in range(CHUNKS):
        send(1, 0, c)
    take_a(5)
    take_a(6)
    qall.wait_recv()
    q1 = qs[QTOT : QTOT + Q1]
    q2 = jnp.concatenate([qs[Q4 + Q3 : QTOT], rq[1, Q4 + Q3 : QTOT]], axis=0)
    q3 = jnp.concatenate([qs[Q4 : Q4 + Q3]] + [rq[j, Q4 : Q4 + Q3] for j in range(1, 4)], axis=0)
    q4 = jnp.concatenate([qs[0:Q4]] + [rq[j, 0:Q4] for j in range(1, LINES)], axis=0)
    arrive(0, 3)
    take_a(far)

    pick = onehot(iota((STATS, 1), 0), iota((1, HD), 1))
    mine = {}
    def line(b, qq, kb):
        m, l, a = attend(qq, kb[...])
        n, base, lines = PICK[b], PBASE[b], 1 << (b - 1)
        mine[b] = (m[:n], l[:n], a[:n])
        stats = pack(m, l)
        for j in range(1, lines):
            part = slice(j * n, (j + 1) * n)
            ps[j, base : base + n] = a[part].astype(BF)
            ps[j, base + n : base + n + STATS, :n] = turn(pick, stats[part]).astype(BF)
        for j in range(lines // 2, lines):
            k = prefix_part(j)
            remote(
                ps.at[j, pl.ds(0, k)], ro.at[j, pl.ds(0, k)], zsend.at[1], zrecv.at[1],
                (xor(z, j) * RING + y, h),
            ).start()

    def keep(res, part):
        m, l, a = part
        res[0] = a
        res[1] = jnp.broadcast_to(m, a.shape)
        res[2] = jnp.broadcast_to(l, a.shape)

    lines = [(4, q4, kb4), (3, q3, kb3), (2, q2, kb2)]
    arrive(1, 0, [lambda args=args: line(*args) for args in lines])
    take_b(0)
    take_b(1)
    take_b(2)
    wall(3, wrecv.at[0]).wait_recv()
    for dx in range(1, 4):
        slot = lax.rem(x + 4 - dx, 4) * 2 + core
        remote(wf.at[slot], wf.at[slot], wsend.at[0], wrecv.at[1], sibling).start()
    arrive(1, 1)
    take_b(3)
    take_b(4)

    half = lax.div(y, 4) * 4
    upper = lax.div(lax.rem(y, 4), 2)

    def tile(t, carry):
        rows = pl.ds(pl.multiple_of(t * 256, 256), 256)
        keys = kb0[pl.ds(half + upper, 3)].reshape(3 * ROWS, 2 * HD)
        m, l, a = attend(qb[rows, :], keys)
        acc0[rows, :] = a
        st0[0, rows, :] = jnp.broadcast_to(m, (256, HD))
        st0[1, rows, :] = jnp.broadcast_to(l, (256, HD))
        return carry

    def tile2(t, carry):
        rows = pl.ds(pl.multiple_of(t * 256, 256), 256)
        part = attend(qb[rows, :], kb0[half + 3 - 3 * upper])
        m, l, a = join([(st0[0, rows, :], st0[1, rows, :], acc0[rows, :]), part])
        acc0[rows, :] = a
        st0[0, rows, :] = m
        st0[1, rows, :] = l
        return carry

    first = []
    arrive(
        1, 2,
        [lambda: tile(0, 0), lambda: tile(1, 0), lambda: first.append(attend(q1, kb1[0 : 5 * Q1]))],
    )
    take_b(5)
    take_b(6)
    lax.fori_loop(0, 2, tile2, 0)
    second = attend(q1, kb1[5 * Q1 : 7 * Q1])
    pall.wait_recv()
    for b, res in ((2, res2), (3, res3), (4, res4)):
        n, base = PICK[b], PBASE[b]
        parts = [unpack(ro[j, base : base + n + STATS], n) for j in range(1, 1 << (b - 1))]
        keep(res, join([mine[b]] + parts))
    def blend(rows, c, group):
        m0, l0, a0 = st0[0, rows, :], st0[1, rows, :], acc0[rows, :]
        place_of = iota((BLK, HD), 0)
        spread = []
        top = m0
        for b, res in group:
            per = PER[b]
            part = pl.ds(pl.multiple_of(c * per, per), per)
            a, m, l = (jnp.concatenate([res[i, part, :]] * (1 << b), axis=0) for i in range(3))
            chosen = (place_of >> (per.bit_length() - 1)) == revs[b]
            m = jnp.where(chosen, m, m0)
            top = jnp.maximum(top, m)
            spread.append((chosen, m, l, a))
        w = jnp.exp2((m0 - top) * COEF)
        den, num = w * l0, w * a0
        for chosen, m, l, a in spread:
            w = jnp.where(chosen, jnp.exp2((m - top) * COEF), 0.0)
            den = den + w * l
            num = num + w * a
        return top, den, num

    def premerge(c, carry):
        rows = pl.ds(pl.multiple_of(c * BLK, BLK), BLK)
        top, den, num = blend(rows, c, ((1, res1), (2, res2), (3, res3), (4, res4)))
        st0[0, rows, :] = top
        st0[1, rows, :] = den
        acc0[rows, :] = num
        return carry

    keep(res1, join([first[0], second]))
    lax.fori_loop(0, NBLK, premerge, 0)
    arrive(1, 3)
    keep(res1, attend(q1, take_b(far)))

    piece = ROWS // HEADS

    def hand(to, dx):
        rows = pl.ds(pl.multiple_of(to * piece, piece), piece)
        remote(att.at[rows], ag.at[h], asem.at[0], asem.at[1 + dx], (s_idx, to)).start()

    for dx in (2, 1, 3, 0):
        c = lax.rem(x + dx, 4)
        rows = pl.ds(pl.multiple_of(c * BLK, BLK), BLK)
        _, den, num = blend(rows, c, ((1, res1),))
        att[rows, :] = mat(back, (num / den).astype(BF)).astype(BF)
        if dx:
            hand(c * 2 + core, dx)
        hand(c * 2 + 1 - core, dx)

    ag[h] = att[pl.ds(pl.multiple_of(h * piece, piece), piece), :]
    wall(4, wrecv.at[1]).wait_recv()
    wall(7, wrecv.at[1]).wait_send()
    qall.wait_send()
    pall.wait_send()
    moved = rings.at[:, pl.ds(0, 7)]
    remote(moved, moved, ysend.at[0], yrecv.at[0], flow_peer[0]).wait_send()
    def product(dx):
        block = ag.at[pl.ds(0, 2 if dx else 1)]
        remote(block, block, asem.at[0], asem.at[1 + dx], sibling).wait_recv()
        pair = pl.ds(lax.rem(x + 4 - dx, 4) * 2, 2)
        lhs = ag[pair]
        lhs = jnp.concatenate([lhs[0], lhs[1]], axis=1)
        return mat(lhs, wf[pair].reshape(2 * HD, HEADS * HD))

    mixed = product(0)
    for dx in (1, 3, 2):
        mixed = mixed + product(dx)
    out_ref[...] = mixed.astype(BF)
    remote(ag.at[pl.ds(0, 7)], ag.at[pl.ds(0, 7)], asem.at[0], asem.at[1], sibling).wait_send()


def on_device(tokens, w_qkv, w_out, offsets):
    hbm = pl.BlockSpec(memory_space=pltpu.HBM)
    dma = pltpu.SemaphoreType.DMA
    vm = pltpu.VMEM
    return pl.pallas_call(
        kernel,
        out_shape=jax.ShapeDtypeStruct((ROWS // HEADS, HEADS * HD), BF),
        in_specs=[hbm] * 4,
        out_specs=pl.BlockSpec(memory_space=pltpu.VMEM),
        scratch_shapes=[
            pltpu.SMEM((NB, HEADS), I32),
            vm((ROWS, HEADS * HD), BF),
            vm((HEADS * HD, 2 * HD), BF),
            vm((HEADS * HD, HD), BF),
            vm((HD, HEADS * HD), BF),
            vm((2, RING, HALF, 2 * HD), BF),
            vm((QTOT + Q1, ROWS), BF),
            vm((QTOT, HALF), BF),
            vm((Q1, ROWS), BF),
            vm((RING, ROWS, 2 * HD), BF),
            vm(((RING - 1) * Q1, 2 * HD), BF),
            *(vm((RING * PICK[b], 2 * HD), BF) for b in range(2, NB)),
            vm((ROWS, HD), BF),
            vm((QTOT + Q1, HD), BF),
            vm((LINES, QTOT, HD), BF),
            vm((LINES, PTOT, HD), BF),
            vm((LINES, PTOT, HD), BF),
            vm((ROWS, HD), BF),
            vm((HEADS, ROWS // HEADS, HD), BF),
            vm((HEADS, HD, HEADS * HD), BF),
            vm((PALL, HD), BF),
            vm((ROWS, HD), F32),
            vm((2, ROWS, HD), F32),
            *(vm((3, PICK[b], HD), F32) for b in range(1, NB)),
            dma((8,)),
            dma((1,)),
            dma((56,)),
            dma((2,)),
            dma((2,)),
            dma((1,)),
            dma((2,)),
            dma((5,)),
        ],
        compiler_params=pltpu.CompilerParams(
            collective_id=0, has_side_effects=True, vmem_limit_bytes=50 * 1024 * 1024
        ),
    )(*(pltpu.with_memory_space_constraint(v, pltpu.HBM) for v in (offsets, tokens, w_qkv, w_out)))


def solution(mesh):
    in_specs = (P("seq", None), P(None, "head"), P("head", None), P())
    out_specs = P(("seq", "head"), None)
    return jax.shard_map(
        on_device, mesh=mesh, in_specs=in_specs, out_specs=out_specs, check_vma=False
    )
```

```python
import math

import jax
import jax.numpy as jnp
from jax import lax
from jax.experimental import pallas as pl
from jax.experimental.pallas import tpu as pltpu
from jax.sharding import PartitionSpec as P

HD = 128
NB = 5
RING = 8
LINES = 8
HEADS = 8
ROWS = 512
RES = 16
BLK = 128
NBLK = ROWS // BLK
HALF = ROWS // 2
CHUNKS = 4
CH = HALF // CHUNKS
PICK = [ROWS >> b for b in range(NB)]
PER = [BLK >> b for b in range(NB)]
Q4, Q3, Q2, Q1 = PICK[4], PICK[3], PICK[2], PICK[1]
QTOT = Q4 + Q3 + Q2
BASE = {4: 0, 3: Q4, 2: Q4 + Q3, 1: QTOT}
COEF = math.log2(math.e) / math.sqrt(HD)
MESH = pl.DeviceIdType.MESH
BF = jnp.bfloat16
F32 = jnp.float32
I32 = jnp.int32


STATS = 16
PBASE = {4: 0, 3: Q4 + STATS, 2: Q4 + Q3 + 2 * STATS}
PTOT = QTOT + 3 * STATS


def prefix(j):
    return QTOT if j == 1 else (Q4 + Q3 if j < 4 else Q4)


def prefix_part(j):
    return PTOT if j == 1 else (PBASE[2] if j < 4 else PBASE[3])


QALL = sum(prefix(j) for j in range(1, LINES))
PALL = sum(prefix_part(j) for j in range(1, LINES))


def xor(a, j):
    out = 0
    for bit in range(3):
        low = lax.rem(lax.div(a, 1 << bit), 2)
        out = out + ((1 - low) if (j >> bit) & 1 else low) * (1 << bit)
    return out


def iota(shape, dim):
    return lax.broadcasted_iota(I32, shape, dim)


def home(i):
    g, k = i >> 3, i & 7
    res = ((g & 1) << 3) | ((g & 2) << 1) | ((g & 4) >> 1) | (g >> 3)
    return k * RES + res


def onehot(a, b):
    return jnp.where(a == b, 1.0, 0.0).astype(BF)


def mat(a, b):
    return jnp.dot(a, b, preferred_element_type=F32)


def attend(q, kv):
    s = lax.dot_general(q, kv[:, :HD], (((1,), (1,)), ((), ())), preferred_element_type=F32)
    m = jnp.max(s, axis=1, keepdims=True)
    p = jnp.exp2((s - m) * COEF)
    l = jnp.sum(p, axis=1, keepdims=True)
    return m, l, mat(p.astype(BF), kv[:, HD:])


def join(parts):
    top = parts[0][0]
    for m, _, _ in parts[1:]:
        top = jnp.maximum(top, m)
    den, num = 0.0, 0.0
    for m, l, a in parts:
        w = jnp.exp2((m - top) * COEF)
        den = den + w * l
        num = num + w * a
    return top, den, num


def three(x):
    hi = x.astype(BF).astype(F32)
    mid = (x - hi).astype(BF).astype(F32)
    return hi, mid, x - hi - mid


def pack(m, l):
    lane = iota((m.shape[0], HD), 1)
    out = jnp.zeros((m.shape[0], HD), F32)
    for i, part in enumerate(three(m) + three(l)):
        out = jnp.where(lane == i, part, out)
    return out.astype(BF)


def turn(a, b):
    return lax.dot_general(a, b, (((1,), (1,)), ((), ())), preferred_element_type=F32)


def unpack(block, n):
    a = block[:n].astype(F32)
    t = turn(onehot(iota((n, 1), 0), iota((1, n), 1)), block[n : n + STATS, :n])
    m = t[:, 0:1] + (t[:, 1:2] + t[:, 2:3])
    l = t[:, 3:4] + (t[:, 4:5] + t[:, 5:6])
    return m, l, a


def kernel(
    off_hbm, tok_hbm, wqkv_hbm, wout_hbm, out_ref,
    off, tok, wkv, wq, wout, rings, selq, sela, selb, kb0, kb1, kb2, kb3, kb4, qb, qs, rq, ps, ro,
    att, ag, wf, spare, acc0, st0, res1, res2, res3, res4,
    insem, ysend, yrecv, zsend, zrecv, wsend, wrecv, asem,
):
    s_idx = lax.axis_index("seq")
    h = lax.axis_index("head")
    z, y = lax.div(s_idx, RING), lax.rem(s_idx, RING)
    x, core = lax.div(h, 2), lax.rem(h, 2)

    loads = [
        (off_hbm, off),
        (wqkv_hbm.at[:, pl.ds(HD, 2 * HD)], wkv),
        *((tok_hbm.at[pl.ds(c * BLK, BLK)], tok.at[pl.ds(c * BLK, BLK)]) for c in range(4)),
        (wqkv_hbm.at[:, pl.ds(0, HD)], wq),
        (wout_hbm, wout),
    ]
    loads = [pltpu.make_async_copy(a, b, insem.at[i]) for i, (a, b) in enumerate(loads)]
    for copy in loads:
        copy.start()

    def at_y(d):
        return z * RING + lax.rem(y + RING + d, RING)

    barrier = pltpu.get_barrier_semaphore()
    peers = [(at_y(-1), h), (at_y(1), h)]
    peers += [(xor(z, j) * RING + y, h) for j in range(1, LINES)]
    peers += [(s_idx, xor(h, j)) for j in range(1, HEADS)]
    for peer in peers:
        pl.semaphore_signal(barrier, inc=1, device_id=peer, device_id_type=MESH)

    def remote(src, dst, send, recv, peer):
        return pltpu.make_async_remote_copy(
            src_ref=src, dst_ref=dst, send_sem=send, recv_sem=recv,
            device_id=peer, device_id_type=MESH,
        )

    loads[0].wait()
    offs = [off[b, h] for b in range(NB)]
    revs = [0]
    for b in range(1, NB):
        rev = 0
        for bit in range(b):
            rev = rev * 2 + lax.rem(lax.div(offs[b], 1 << bit), 2)
        revs.append(rev)
    wanted = []
    for rho in range(RES):
        hit = (offs[4] == rho) | (offs[3] == rho % 8) | (offs[2] == rho % 4)
        wanted.append(jnp.where(hit, 1, 0))
    total = sum(wanted)
    ranks, before = [], 0
    for rho in range(RES):
        ranks.append(before * wanted[rho] + (total + rho - before) * (1 - wanted[rho]))
        before = before + wanted[rho]

    lane = iota((1, BLK), 1)
    rank = jnp.zeros((1, BLK), I32)
    for rho in range(RES):
        rank = jnp.where((lane & 15) == rho, ranks[rho], rank)
    travel = onehot(iota((BLK, 1), 0), rank * 8 + (lane >> 4))

    own, sides, far = 0, [[1, 3, 5], [2, 4, 6]], 7
    flow_peer = [(at_y(-1), h), (at_y(1), h)]

    def ring(ph, d, hop, c):
        slots = [own] + sides[d] + [far]
        rows = pl.ds(c * CH, CH)
        recv = yrecv.at[(ph * 2 + d) * 14 + (hop * CHUNKS + c if hop < 3 else 12 + c % 2)]
        return remote(
            rings.at[ph, slots[hop], rows], rings.at[ph, slots[hop + 1], rows],
            ysend.at[0], recv, flow_peer[d],
        )

    def last(d):
        return range(CHUNKS // 2) if d == 0 else range(CHUNKS // 2, CHUNKS)

    def send(ph, hop, c):
        for d in range(2):
            ring(ph, d, hop, c).start()

    def arrive(ph, hop, fill=()):
        for c in range(CHUNKS):
            for d in range(2):
                if hop < 3 or c in last(d):
                    ring(ph, d, hop, c).wait_recv()
                    if hop < 2 or (hop == 2 and c in last(d)):
                        ring(ph, d, hop + 1, c).start()
            if c < len(fill):
                fill[c]()

    loads[1].wait()
    for c in range(CHUNKS):
        loads[2 + c].wait()
        kv = mat(tok[c * BLK : (c + 1) * BLK], wkv[...]).astype(BF)
        for i in range(1):
            part = mat(travel, kv[i * BLK : (i + 1) * BLK]).astype(BF)
            at = c * CH + i * (BLK // 2)
            rings[0, own, at : at + BLK // 2] = part[: BLK // 2]
            rings[1, own, at : at + BLK // 2] = part[BLK // 2 :]
        if c == 0:
            pl.semaphore_wait(barrier, len(peers))
        send(0, 0, c)

    place = iota((1, ROWS), 1)
    group = ((place >> 3) & 7) + ((place >> 8) << 3)
    label = jnp.zeros((1, ROWS), I32)
    for rho in range(RES):
        label = jnp.where(group == ranks[rho], rho, label)
    label = label * 32 + ((place >> 6) & 3) * 8 + (place & 7)
    for b in range(NB - 1, 0, -1):
        n = PICK[b]
        row = iota((n, 1), 0)
        key = (offs[b] + (row >> 5) * (1 << b)) * 32 + (row & 31)
        if b > 1:
            sela[BASE[b] : BASE[b] + n] = onehot(key, label[:, :HALF])
        else:
            selb[...] = onehot(key, label)
    static = onehot(home(iota((BLK, 1), 0)), iota((1, BLK), 1))
    back = onehot(iota((BLK, 1), 0), home(iota((1, BLK), 1)))

    loads[6].wait()
    for c in range(NBLK):
        rows = slice(c * BLK, (c + 1) * BLK)
        qb[rows] = mat(static, mat(tok[rows], wq[...]).astype(BF)).astype(BF)
    for b in range(NB - 1, 0, -1):
        n, per = PICK[b], PER[b]
        row = iota((n, 1), 0)
        shift = per.bit_length() - 1
        key = (row >> shift) * BLK + revs[b] * per + (row & (per - 1))
        selq[BASE[b] : BASE[b] + n] = onehot(key, place)
    qs[...] = mat(selq[...], qb[...]).astype(BF)
    for j in range(1, LINES):
        n = prefix(j)
        remote(
            qs.at[pl.ds(0, n)], rq.at[j, pl.ds(0, n)], zsend.at[0], zrecv.at[0],
            (xor(z, j) * RING + y, h),
        ).start()
    qall = remote(spare.at[pl.ds(0, QALL)], spare.at[pl.ds(0, QALL)], zsend.at[0], zrecv.at[0], peers[2])
    pall = remote(spare, spare, zsend.at[1], zrecv.at[1], peers[2])

    signed = [0, 1, -1, 2, -2, 3, -3, 4]

    def take_a(slot):
        block = rings[0, slot]
        if slot != far:
            kb0[lax.rem(y + RING + signed[slot], RING), 0:HALF] = block
        taken = mat(sela[...], block).astype(BF)
        for b, buf in ((2, kb2), (3, kb3), (4, kb4)):
            n = PICK[b]
            buf[slot * n : (slot + 1) * n] = taken[BASE[b] : BASE[b] + n]

    def take_b(slot):
        block = rings[1, slot]
        if slot != far:
            kb0[lax.rem(y + RING + signed[slot], RING), HALF:ROWS] = block
        both = mat(selb[:, :HALF], rings[0, slot]) + mat(selb[:, HALF:], block)
        if slot == far:
            return both.astype(BF)
        kb1[slot * Q1 : (slot + 1) * Q1] = both.astype(BF)

    arrive(0, 0)

    loads[7].wait()
    for dx in range(1, 4):
        to = (s_idx, lax.rem(x + dx, 4) * 2 + core)
        remote(wout, wf.at[h], wsend.at[0], wrecv.at[0], to).start()
    sibling = (s_idx, x * 2 + 1 - core)
    remote(wout, wf.at[h], wsend.at[0], wrecv.at[1], sibling).start()
    wf[h] = wout[...]

    def wall(n, sem):
        return remote(wf.at[pl.ds(0, n)], wf.at[pl.ds(0, n)], wsend.at[0], sem, sibling)

    take_a(0)
    take_a(1)
    take_a(2)
    arrive(0, 1)
    for c in range(CHUNKS):
        send(1, 0, c)
    take_a(3)
    take_a(4)
    arrive(0, 2)
    take_a(5)
    take_a(6)
    qall.wait_recv()
    q1 = qs[QTOT : QTOT + Q1]
    q2 = jnp.concatenate([qs[Q4 + Q3 : QTOT], rq[1, Q4 + Q3 : QTOT]], axis=0)
    q3 = jnp.concatenate([qs[Q4 : Q4 + Q3]] + [rq[j, Q4 : Q4 + Q3] for j in range(1, 4)], axis=0)
    q4 = jnp.concatenate([qs[0:Q4]] + [rq[j, 0:Q4] for j in range(1, LINES)], axis=0)
    arrive(0, 3)
    take_a(far)

    pick = onehot(iota((STATS, 1), 0), iota((1, HD), 1))
    mine = {}
    def line(b, qq, kb):
        m, l, a = attend(qq, kb[...])
        n, base, lines = PICK[b], PBASE[b], 1 << (b - 1)
        mine[b] = (m[:n], l[:n], a[:n])
        stats = pack(m, l)
        for j in range(1, lines):
            part = slice(j * n, (j + 1) * n)
            ps[j, base : base + n] = a[part].astype(BF)
            ps[j, base + n : base + n + STATS, :n] = turn(pick, stats[part]).astype(BF)
        for j in range(lines // 2, lines):
            k = prefix_part(j)
            remote(
                ps.at[j, pl.ds(0, k)], ro.at[j, pl.ds(0, k)], zsend.at[1], zrecv.at[1],
                (xor(z, j) * RING + y, h),
            ).start()

    def keep(res, part):
        m, l, a = part
        res[0] = a
        res[1] = jnp.broadcast_to(m, a.shape)
        res[2] = jnp.broadcast_to(l, a.shape)

    lines = [(4, q4, kb4), (3, q3, kb3), (2, q2, kb2)]
    arrive(1, 0, [lambda args=args: line(*args) for args in lines])
    take_b(0)
    take_b(1)
    take_b(2)
    wall(3, wrecv.at[0]).wait_recv()
    for dx in range(1, 4):
        slot = lax.rem(x + 4 - dx, 4) * 2 + core
        remote(wf.at[slot], wf.at[slot], wsend.at[0], wrecv.at[1], sibling).start()
    arrive(1, 1)
    take_b(3)
    take_b(4)

    half = lax.div(y, 4) * 4
    upper = lax.div(lax.rem(y, 4), 2)

    def tile(t, carry):
        rows = pl.ds(pl.multiple_of(t * 256, 256), 256)
        keys = kb0[pl.ds(half + upper, 3)].reshape(3 * ROWS, 2 * HD)
        m, l, a = attend(qb[rows, :], keys)
        acc0[rows, :] = a
        st0[0, rows, :] = jnp.broadcast_to(m, (256, HD))
        st0[1, rows, :] = jnp.broadcast_to(l, (256, HD))
        return carry

    def tile2(t, carry):
        rows = pl.ds(pl.multiple_of(t * 256, 256), 256)
        part = attend(qb[rows, :], kb0[half + 3 - 3 * upper])
        m, l, a = join([(st0[0, rows, :], st0[1, rows, :], acc0[rows, :]), part])
        acc0[rows, :] = a
        st0[0, rows, :] = m
        st0[1, rows, :] = l
        return carry

    first = []
    arrive(
        1, 2,
        [lambda: tile(0, 0), lambda: tile(1, 0), lambda: first.append(attend(q1, kb1[0 : 5 * Q1]))],
    )
    take_b(5)
    take_b(6)
    lax.fori_loop(0, 2, tile2, 0)
    second = attend(q1, kb1[5 * Q1 : 7 * Q1])
    pall.wait_recv()
    for b, res in ((2, res2), (3, res3), (4, res4)):
        n, base = PICK[b], PBASE[b]
        parts = [unpack(ro[j, base : base + n + STATS], n) for j in range(1, 1 << (b - 1))]
        keep(res, join([mine[b]] + parts))
    def blend(rows, c, group):
        m0, l0, a0 = st0[0, rows, :], st0[1, rows, :], acc0[rows, :]
        place_of = iota((BLK, HD), 0)
        spread = []
        top = m0
        for b, res in group:
            per = PER[b]
            part = pl.ds(pl.multiple_of(c * per, per), per)
            a, m, l = (jnp.concatenate([res[i, part, :]] * (1 << b), axis=0) for i in range(3))
            chosen = (place_of >> (per.bit_length() - 1)) == revs[b]
            m = jnp.where(chosen, m, m0)
            top = jnp.maximum(top, m)
            spread.append((chosen, m, l, a))
        w = jnp.exp2((m0 - top) * COEF)
        den, num = w * l0, w * a0
        for chosen, m, l, a in spread:
            w = jnp.where(chosen, jnp.exp2((m - top) * COEF), 0.0)
            den = den + w * l
            num = num + w * a
        return top, den, num

    def premerge(c, carry):
        rows = pl.ds(pl.multiple_of(c * BLK, BLK), BLK)
        top, den, num = blend(rows, c, ((1, res1), (2, res2), (3, res3), (4, res4)))
        st0[0, rows, :] = top
        st0[1, rows, :] = den
        acc0[rows, :] = num
        return carry

    keep(res1, join([first[0], second]))
    lax.fori_loop(0, NBLK, premerge, 0)
    arrive(1, 3)
    keep(res1, attend(q1, take_b(far)))

    piece = ROWS // HEADS

    def hand(to, dx):
        rows = pl.ds(pl.multiple_of(to * piece, piece), piece)
        remote(att.at[rows], ag.at[h], asem.at[0], asem.at[1 + dx], (s_idx, to)).start()

    for dx in (2, 1, 3, 0):
        c = lax.rem(x + dx, 4)
        rows = pl.ds(pl.multiple_of(c * BLK, BLK), BLK)
        _, den, num = blend(rows, c, ((1, res1),))
        att[rows, :] = mat(back, (num / den).astype(BF)).astype(BF)
        if dx:
            hand(c * 2 + core, dx)
        hand(c * 2 + 1 - core, dx)

    ag[h] = att[pl.ds(pl.multiple_of(h * piece, piece), piece), :]
    wall(4, wrecv.at[1]).wait_recv()
    wall(7, wrecv.at[1]).wait_send()
    qall.wait_send()
    pall.wait_send()
    moved = rings.at[:, pl.ds(0, 7)]
    remote(moved, moved, ysend.at[0], yrecv.at[0], flow_peer[0]).wait_send()
    def product(dx):
        block = ag.at[pl.ds(0, 2 if dx else 1)]
        remote(block, block, asem.at[0], asem.at[1 + dx], sibling).wait_recv()
        pair = pl.ds(lax.rem(x + 4 - dx, 4) * 2, 2)
        lhs = ag[pair]
        lhs = jnp.concatenate([lhs[0], lhs[1]], axis=1)
        return mat(lhs, wf[pair].reshape(2 * HD, HEADS * HD))

    mixed = product(0)
    for dx in (1, 3, 2):
        mixed = mixed + product(dx)
    out_ref[...] = mixed.astype(BF)
    remote(ag.at[pl.ds(0, 7)], ag.at[pl.ds(0, 7)], asem.at[0], asem.at[1], sibling).wait_send()


def on_device(tokens, w_qkv, w_out, offsets):
    hbm = pl.BlockSpec(memory_space=pltpu.HBM)
    dma = pltpu.SemaphoreType.DMA
    vm = pltpu.VMEM
    return pl.pallas_call(
        kernel,
        out_shape=jax.ShapeDtypeStruct((ROWS // HEADS, HEADS * HD), BF),
        in_specs=[hbm] * 4,
        out_specs=pl.BlockSpec(memory_space=pltpu.VMEM),
        scratch_shapes=[
            pltpu.SMEM((NB, HEADS), I32),
            vm((ROWS, HEADS * HD), BF),
            vm((HEADS * HD, 2 * HD), BF),
            vm((HEADS * HD, HD), BF),
            vm((HD, HEADS * HD), BF),
            vm((2, RING, HALF, 2 * HD), BF),
            vm((QTOT + Q1, ROWS), BF),
            vm((QTOT, HALF), BF),
            vm((Q1, ROWS), BF),
            vm((RING, ROWS, 2 * HD), BF),
            vm(((RING - 1) * Q1, 2 * HD), BF),
            *(vm((RING * PICK[b], 2 * HD), BF) for b in range(2, NB)),
            vm((ROWS, HD), BF),
            vm((QTOT + Q1, HD), BF),
            vm((LINES, QTOT, HD), BF),
            vm((LINES, PTOT, HD), BF),
            vm((LINES, PTOT, HD), BF),
            vm((ROWS, HD), BF),
            vm((HEADS, ROWS // HEADS, HD), BF),
            vm((HEADS, HD, HEADS * HD), BF),
            vm((PALL, HD), BF),
            vm((ROWS, HD), F32),
            vm((2, ROWS, HD), F32),
            *(vm((3, PICK[b], HD), F32) for b in range(1, NB)),
            dma((8,)),
            dma((1,)),
            dma((56,)),
            dma((2,)),
            dma((2,)),
            dma((1,)),
            dma((2,)),
            dma((5,)),
        ],
        compiler_params=pltpu.CompilerParams(
            collective_id=0, has_side_effects=True, vmem_limit_bytes=50 * 1024 * 1024
        ),
    )(*(pltpu.with_memory_space_constraint(v, pltpu.HBM) for v in (offsets, tokens, w_qkv, w_out)))


def solution(mesh):
    in_specs = (P("seq", None), P(None, "head"), P("head", None), P())
    out_specs = P(("seq", "head"), None)
    return jax.shard_map(
        on_device, mesh=mesh, in_specs=in_specs, out_specs=out_specs, check_vma=False
    )
```
